128 devices in a mesh: smp: 32 (over x, z, y_lo), col: 2 (over core), slab: 2 (over y_hi).
Axes of the slice: x: 4, y: 4 (y_hi: 2, y_lo: 2; y = y_hi * 2 + y_lo), z: 4, core: 2. Of those that a mesh axis runs over, the one named last changes fastest.
Arguments:
- jacobian: bfloat16 [1024, 32, 16384], P('smp', 'slab', 'col'), may hold values from -0.005722046 to 0.005722046
- local_energy: float32 [1024], P('smp'), may hold values from -6 to 6
Outputs:
- update: float32 [32, 16384], P('slab', ('col', 'smp'))
The draws below stay inside these ranges and needn't reach their ends.
All inputs are finite; a program needn't handle non-finite values.
Results may differ from the reference program's by a relative error of at most 0.0085.
Values may be sent and summed in bfloat16 or wider, within the bound.
A program may use at most 192 MiB of HBM per device.

```python
import jax
import jax.numpy as jnp
from jax import lax

SLABS = 32
SLAB_COLS = 16384
NS = 1024
PARAMS = 524288


def draw_jacobian(key, part):
    band_width = 16
    groups = NS // band_width + 1
    row_scale = jnp.exp(jax.random.uniform(jax.random.fold_in(key, 7), (NS,)) * jnp.log(10.0))
    sample_ids = jnp.arange(NS, dtype=jnp.int32)

    def one_slab(index):
        slab_key = jax.random.fold_in(key, index + 100)
        keys = jax.random.split(slab_key, 4)
        offsets = jax.random.randint(keys[1], (SLAB_COLS,), 0, band_width)
        group_ids = (sample_ids[:, None] + offsets[None, :]) // band_width
        noise = jnp.clip(jax.random.normal(keys[0], (NS, SLAB_COLS)), -5.0, 5.0)
        shared = jnp.clip(jax.random.normal(keys[2], (groups, SLAB_COLS)), -5.0, 5.0)
        picked = jnp.take_along_axis(shared, group_ids, axis=0)
        position = (index * SLAB_COLS + jnp.arange(SLAB_COLS)).astype(jnp.float32) / (SLABS * SLAB_COLS)
        col_scale = jnp.exp(jax.random.uniform(keys[3], (SLAB_COLS,)) * jnp.log(10.0)) * (1.0 + 2.0 * position)
        values = (noise + picked) * row_scale[:, None] * col_scale[None, :] / (SLABS * SLAB_COLS)
        return values.astype(jnp.bfloat16)
    stacked = lax.map(one_slab, jnp.arange(SLABS, dtype=jnp.int32))
    return jnp.moveaxis(stacked, 0, 1)


def shard_levels(rng, extent, cuts, low, top_value):
    factor_of = 1.0
    for dim, shards_of in cuts:
        draws = jax.random.uniform(jax.random.fold_in(jax.random.fold_in(rng, 6), dim), (shards_of,), jnp.float32, low / len(cuts), top_value / len(cuts))
        factor_of = factor_of * jnp.repeat(jnp.exp(draws), extent[dim] // shards_of).reshape((-1,) + (1,) * (len(extent) - 1 - dim))
    return factor_of


def scatter_about(rng, shape, deviation, bound, cuts=(), kind=jnp.bfloat16):
    gain = shard_levels(rng, shape, cuts, -0.22, 0.18) if cuts else 1.0
    entries = jax.random.normal(rng, shape, jnp.float32) * deviation * gain
    return jnp.minimum(jnp.maximum(entries, -bound), bound).astype(kind)


def setup_inputs(seed: int = 0) -> dict:
    streams_of = jax.random.split(jax.random.key(seed), 3)
    return {
        "jacobian": draw_jacobian(jax.random.fold_in(streams_of[2], 71), 0),
        "local_energy": scatter_about(streams_of[1], (NS,), 1.0, 6.0, ((0, 32),), jnp.float32),
    }


def center_slab(slab):
    values = slab.astype(jnp.float32)
    mean_row = lax.optimization_barrier(jnp.mean(values, axis=0, keepdims=True))
    return ((values - mean_row) / jnp.sqrt(jnp.float32(NS))).astype(jnp.bfloat16)

def reference(jacobian, local_energy):
    eps = (local_energy - jnp.mean(local_energy)) / jnp.sqrt(jnp.float32(NS))
    slabs_first = jnp.moveaxis(jacobian, 1, 0)

    def add_gram(total, slab):
        centered = center_slab(slab)
        return (total + jnp.dot(centered.astype(jnp.float32), centered.T.astype(jnp.float32), preferred_element_type=jnp.float32), None)
    gram, unused = lax.scan(add_gram, jnp.zeros((NS, NS), jnp.float32), slabs_first)
    shift = 0.01 * jnp.trace(gram) / NS
    factor = jnp.linalg.cholesky(gram + shift * jnp.eye(NS, dtype=jnp.float32))
    middle = lax.linalg.triangular_solve(factor, eps[:, None], left_side=True, lower=True)
    coeffs = lax.linalg.triangular_solve(factor, middle, left_side=True, lower=True, transpose_a=True)[:, 0]

    def slab_delta(carry, slab):
        centered = center_slab(slab).astype(jnp.float32)
        return (carry, jnp.dot(coeffs, centered, precision=lax.Precision.HIGHEST))
    unused, delta = lax.scan(slab_delta, jnp.float32(0.0), slabs_first)
    size = jnp.sqrt(jnp.sum(delta * delta))
    limit = 0.3 * jnp.sqrt(jnp.float32(PARAMS))
    return -jnp.minimum(1.0, limit / size) * delta
```

```python
import jax
import jax.numpy as jnp
from jax import lax
from jax.sharding import PartitionSpec as P

SLABS = 32
SLAB_COLS = 16384


def shards(jacobian, local_energy):
    energies = lax.all_gather(local_energy, "smp", axis=0, tiled=True)
    jacobian, energies = lax.optimization_barrier((jacobian, energies))
    samples = energies.shape[0]
    root_count = jnp.sqrt(jnp.float32(samples))
    eps = (energies - jnp.mean(energies)) / root_count
    columns = lax.all_to_all(jacobian, "smp", split_axis=2, concat_axis=0, tiled=True)
    slab_count = columns.shape[1]
    width = columns.shape[2]
    values = columns.astype(jnp.float32)
    mean_row = jnp.mean(values, axis=0, keepdims=True)
    centered = (
        ((values - mean_row) / root_count).astype(jnp.bfloat16).reshape(samples, slab_count * width)
    )
    partial_gram = jnp.dot(centered, centered.T, preferred_element_type=jnp.float32)
    gram = lax.psum(partial_gram, ("smp", "col", "slab"))
    shift = 0.01 * jnp.trace(gram) / samples
    factor = jnp.linalg.cholesky(gram + shift * jnp.eye(samples, dtype=jnp.float32))
    middle = lax.linalg.triangular_solve(factor, eps[:, None], left_side=True, lower=True)
    coeffs = lax.linalg.triangular_solve(
        factor, middle, left_side=True, lower=True, transpose_a=True
    )[:, 0]
    delta = jnp.dot(coeffs, centered.astype(jnp.float32), precision=lax.Precision.HIGHEST)
    squared = jnp.dot(coeffs, jnp.dot(gram, coeffs, precision=lax.Precision.HIGHEST),
                      precision=lax.Precision.HIGHEST)
    limit = 0.3 * jnp.sqrt(jnp.float32(SLABS * SLAB_COLS))
    scaled = -jnp.minimum(1.0, limit / jnp.sqrt(squared)) * delta
    return scaled.reshape(slab_count, width)


def solution(mesh):
    in_specs = (P("smp", "slab", "col"), P("smp"))
    out_specs = P("slab", ("col", "smp"))
    return jax.shard_map(shards, mesh=mesh, in_specs=in_specs, out_specs=out_specs, check_vma=False)
```

```python
import functools

import jax
import jax.numpy as jnp
from jax import lax
from jax.experimental import pallas as pl
from jax.experimental.pallas import tpu as pltpu
from jax.sharding import PartitionSpec as P

SLABS = 32
SLAB_COLS = 16384


def exchange_kernel(n, width, jac_ref, en_ref, cols_ref, en_all_ref,
                    send_sems, recv_sems, en_send, en_recv, local_sems):
    me = lax.axis_index("smp")
    col = lax.axis_index("col")
    slab = lax.axis_index("slab")

    def piece(t):
        return jac_ref.at[:, :, pl.ds(pl.multiple_of(t * width, width), width)]

    local = pltpu.make_async_copy(piece(me), cols_ref.at[me], local_sems.at[0])
    local.start()
    local_en = pltpu.make_async_copy(en_ref, en_all_ref.at[me], local_sems.at[1])
    local_en.start()
    sends = []
    for k in range(1, n):
        t = lax.rem(me + k, n)
        dev = (t, col, slab)
        c = pltpu.make_async_remote_copy(
            src_ref=piece(t), dst_ref=cols_ref.at[me],
            send_sem=send_sems.at[t], recv_sem=recv_sems.at[me],
            device_id=dev, device_id_type=pl.DeviceIdType.MESH)
        c.start()
        e = pltpu.make_async_remote_copy(
            src_ref=en_ref, dst_ref=en_all_ref.at[me],
            send_sem=en_send.at[t], recv_sem=en_recv.at[me],
            device_id=dev, device_id_type=pl.DeviceIdType.MESH)
        e.start()
        sends.append((c, e))
    for k in range(1, n):
        s = lax.rem(me + n - k, n)
        dev = (s, col, slab)
        pltpu.make_async_remote_copy(
            src_ref=piece(me), dst_ref=cols_ref.at[s],
            send_sem=send_sems.at[s], recv_sem=recv_sems.at[s],
            device_id=dev, device_id_type=pl.DeviceIdType.MESH).wait_recv()
        pltpu.make_async_remote_copy(
            src_ref=en_ref, dst_ref=en_all_ref.at[s],
            send_sem=en_send.at[s], recv_sem=en_recv.at[s],
            device_id=dev, device_id_type=pl.DeviceIdType.MESH).wait_recv()
    for c, e in sends:
        c.wait_send()
        e.wait_send()
    local.wait()
    local_en.wait()


def exchange(jacobian, local_energy, n):
    rows, slabs, cols = jacobian.shape
    width = cols // n
    en = local_energy.reshape(1, rows)
    return pl.pallas_call(
        functools.partial(exchange_kernel, n, width),
        out_shape=(
            jax.ShapeDtypeStruct((n, rows, slabs, width), jacobian.dtype),
            jax.ShapeDtypeStruct((n, 1, rows), local_energy.dtype),
        ),
        in_specs=[pl.BlockSpec(memory_space=pl.ANY)] * 2,
        out_specs=(pl.BlockSpec(memory_space=pl.ANY), pl.BlockSpec(memory_space=pl.ANY)),
        scratch_shapes=[
            pltpu.SemaphoreType.DMA((n,)),
            pltpu.SemaphoreType.DMA((n,)),
            pltpu.SemaphoreType.DMA((n,)),
            pltpu.SemaphoreType.DMA((n,)),
            pltpu.SemaphoreType.DMA((2,)),
        ],
        compiler_params=pltpu.CompilerParams(has_side_effects=True),
    )(jacobian, en)


def shards(n, jacobian, local_energy):
    gathered, energies = exchange(jacobian, local_energy, n)
    energies = energies.reshape(-1)
    samples = energies.shape[0]
    root_count = jnp.sqrt(jnp.float32(samples))
    eps = (energies - jnp.mean(energies)) / root_count
    columns = gathered.reshape(samples, gathered.shape[2], gathered.shape[3])
    slab_count = columns.shape[1]
    width = columns.shape[2]
    values = columns.astype(jnp.float32)
    mean_row = jnp.mean(values, axis=0, keepdims=True)
    centered = (
        ((values - mean_row) / root_count).astype(jnp.bfloat16).reshape(samples, slab_count * width)
    )
    partial_gram = jnp.dot(centered, centered.T, preferred_element_type=jnp.float32)
    gram = lax.psum(partial_gram, ("smp", "col", "slab"))
    shift = 0.01 * jnp.trace(gram) / samples
    factor = jnp.linalg.cholesky(gram + shift * jnp.eye(samples, dtype=jnp.float32))
    middle = lax.linalg.triangular_solve(factor, eps[:, None], left_side=True, lower=True)
    coeffs = lax.linalg.triangular_solve(
        factor, middle, left_side=True, lower=True, transpose_a=True
    )[:, 0]
    delta = jnp.dot(coeffs, centered.astype(jnp.float32), precision=lax.Precision.HIGHEST)
    squared = jnp.dot(coeffs, jnp.dot(gram, coeffs, precision=lax.Precision.HIGHEST),
                      precision=lax.Precision.HIGHEST)
    limit = 0.3 * jnp.sqrt(jnp.float32(SLABS * SLAB_COLS))
    scaled = -jnp.minimum(1.0, limit / jnp.sqrt(squared)) * delta
    return scaled.reshape(slab_count, width)


def solution(mesh):
    in_specs = (P("smp", "slab", "col"), P("smp"))
    out_specs = P("slab", ("col", "smp"))
    return jax.shard_map(functools.partial(shards, mesh.shape["smp"]), mesh=mesh,
                         in_specs=in_specs, out_specs=out_specs, check_vma=False)
```

```python
import functools

import jax
import jax.numpy as jnp
from jax import lax
from jax.experimental import pallas as pl
from jax.experimental.pallas import tpu as pltpu
from jax.sharding import PartitionSpec as P

SLABS = 32
SLAB_COLS = 16384


def exchange_kernel(n, width, jac_ref, en_ref, cols_ref, en_all_ref,
                    send_sems, recv_sems, en_send, en_recv, local_sems):
    me = lax.axis_index("smp")
    col = lax.axis_index("col")
    slab = lax.axis_index("slab")

    def piece(t):
        return jac_ref.at[:, :, pl.ds(pl.multiple_of(t * width, width), width)]

    local = pltpu.make_async_copy(piece(me), cols_ref.at[me], local_sems.at[0])
    local.start()
    local_en = pltpu.make_async_copy(en_ref, en_all_ref.at[me], local_sems.at[1])
    local_en.start()
    sends = []
    for k in range(1, n):
        t = lax.rem(me + k, n)
        dev = (t, col, slab)
        c = pltpu.make_async_remote_copy(
            src_ref=piece(t), dst_ref=cols_ref.at[me],
            send_sem=send_sems.at[t], recv_sem=recv_sems.at[me],
            device_id=dev, device_id_type=pl.DeviceIdType.MESH)
        c.start()
        e = pltpu.make_async_remote_copy(
            src_ref=en_ref, dst_ref=en_all_ref.at[me],
            send_sem=en_send.at[t], recv_sem=en_recv.at[me],
            device_id=dev, device_id_type=pl.DeviceIdType.MESH)
        e.start()
        sends.append((c, e))
    for k in range(1, n):
        s = lax.rem(me + n - k, n)
        dev = (s, col, slab)
        pltpu.make_async_remote_copy(
            src_ref=piece(me), dst_ref=cols_ref.at[s],
            send_sem=send_sems.at[s], recv_sem=recv_sems.at[s],
            device_id=dev, device_id_type=pl.DeviceIdType.MESH).wait_recv()
        pltpu.make_async_remote_copy(
            src_ref=en_ref, dst_ref=en_all_ref.at[s],
            send_sem=en_send.at[s], recv_sem=en_recv.at[s],
            device_id=dev, device_id_type=pl.DeviceIdType.MESH).wait_recv()
    for c, e in sends:
        c.wait_send()
        e.wait_send()
    local.wait()
    local_en.wait()


def exchange(jacobian, local_energy, n):
    rows, slabs, cols = jacobian.shape
    width = cols // n
    en = local_energy.reshape(1, rows)
    return pl.pallas_call(
        functools.partial(exchange_kernel, n, width),
        out_shape=(
            jax.ShapeDtypeStruct((n, rows, slabs, width), jacobian.dtype),
            jax.ShapeDtypeStruct((n, 1, rows), local_energy.dtype),
        ),
        in_specs=[pl.BlockSpec(memory_space=pl.ANY)] * 2,
        out_specs=(pl.BlockSpec(memory_space=pl.ANY), pl.BlockSpec(memory_space=pl.ANY)),
        scratch_shapes=[
            pltpu.SemaphoreType.DMA((n,)),
            pltpu.SemaphoreType.DMA((n,)),
            pltpu.SemaphoreType.DMA((n,)),
            pltpu.SemaphoreType.DMA((n,)),
            pltpu.SemaphoreType.DMA((2,)),
        ],
        compiler_params=pltpu.CompilerParams(has_side_effects=True),
    )(jacobian, en)


def symmetric_psum(partial, axes, block=128):
    size = partial.shape[0]
    nb = size // block
    blocks = partial.reshape(nb, block, nb, block).transpose(0, 2, 1, 3)
    pairs = [(i, j) for i in range(nb) for j in range(i + 1)]
    lower = jnp.stack([blocks[i, j] for i, j in pairs])
    lower = lax.psum(lower, axes)
    where = {p: k for k, p in enumerate(pairs)}
    rows = []
    for i in range(nb):
        row = [lower[where[(i, j)]] if j <= i else lower[where[(j, i)]].T for j in range(nb)]
        rows.append(jnp.concatenate(row, axis=1))
    return jnp.concatenate(rows, axis=0)


def shards(n, jacobian, local_energy):
    gathered, energies = exchange(jacobian, local_energy, n)
    energies = energies.reshape(-1)
    samples = energies.shape[0]
    root_count = jnp.sqrt(jnp.float32(samples))
    eps = (energies - jnp.mean(energies)) / root_count
    columns = gathered.reshape(samples, gathered.shape[2], gathered.shape[3])
    slab_count = columns.shape[1]
    width = columns.shape[2]
    values = columns.astype(jnp.float32)
    mean_row = jnp.mean(values, axis=0, keepdims=True)
    centered = (
        ((values - mean_row) / root_count).astype(jnp.bfloat16).reshape(samples, slab_count * width)
    )
    partial_gram = jnp.dot(centered, centered.T, preferred_element_type=jnp.float32)
    gram = symmetric_psum(partial_gram, ("smp", "col", "slab"))
    shift = 0.01 * jnp.trace(gram) / samples
    factor = jnp.linalg.cholesky(gram + shift * jnp.eye(samples, dtype=jnp.float32))
    middle = lax.linalg.triangular_solve(factor, eps[:, None], left_side=True, lower=True)
    coeffs = lax.linalg.triangular_solve(
        factor, middle, left_side=True, lower=True, transpose_a=True
    )[:, 0]
    delta = jnp.dot(coeffs, centered.astype(jnp.float32), precision=lax.Precision.HIGHEST)
    squared = jnp.dot(coeffs, jnp.dot(gram, coeffs, precision=lax.Precision.HIGHEST),
                      precision=lax.Precision.HIGHEST)
    limit = 0.3 * jnp.sqrt(jnp.float32(SLABS * SLAB_COLS))
    scaled = -jnp.minimum(1.0, limit / jnp.sqrt(squared)) * delta
    return scaled.reshape(slab_count, width)


def solution(mesh):
    in_specs = (P("smp", "slab", "col"), P("smp"))
    out_specs = P("slab", ("col", "smp"))
    return jax.shard_map(functools.partial(shards, mesh.shape["smp"]), mesh=mesh,
                         in_specs=in_specs, out_specs=out_specs, check_vma=False)
```

```python
import functools

import jax
import jax.numpy as jnp
from jax import lax
from jax.experimental import pallas as pl
from jax.experimental.pallas import tpu as pltpu
from jax.sharding import PartitionSpec as P

SLABS = 32
SLAB_COLS = 16384


def exchange_kernel(n, width, jac_ref, en_ref, cols_ref, en_all_ref,
                    send_sems, recv_sems, en_send, en_recv, local_sems):
    me = lax.axis_index("smp")
    col = lax.axis_index("col")
    slab = lax.axis_index("slab")

    def piece(t):
        return jac_ref.at[:, :, pl.ds(pl.multiple_of(t * width, width), width)]

    local = pltpu.make_async_copy(piece(me), cols_ref.at[me], local_sems.at[0])
    local.start()
    local_en = pltpu.make_async_copy(en_ref, en_all_ref.at[me], local_sems.at[1])
    local_en.start()
    sends = []
    for k in range(1, n):
        t = lax.rem(me + k, n)
        dev = (t, col, slab)
        c = pltpu.make_async_remote_copy(
            src_ref=piece(t), dst_ref=cols_ref.at[me],
            send_sem=send_sems.at[t], recv_sem=recv_sems.at[me],
            device_id=dev, device_id_type=pl.DeviceIdType.MESH)
        c.start()
        e = pltpu.make_async_remote_copy(
            src_ref=en_ref, dst_ref=en_all_ref.at[me],
            send_sem=en_send.at[t], recv_sem=en_recv.at[me],
            device_id=dev, device_id_type=pl.DeviceIdType.MESH)
        e.start()
        sends.append((c, e))
    for k in range(1, n):
        s = lax.rem(me + n - k, n)
        dev = (s, col, slab)
        pltpu.make_async_remote_copy(
            src_ref=piece(me), dst_ref=cols_ref.at[s],
            send_sem=send_sems.at[s], recv_sem=recv_sems.at[s],
            device_id=dev, device_id_type=pl.DeviceIdType.MESH).wait_recv()
        pltpu.make_async_remote_copy(
            src_ref=en_ref, dst_ref=en_all_ref.at[s],
            send_sem=en_send.at[s], recv_sem=en_recv.at[s],
            device_id=dev, device_id_type=pl.DeviceIdType.MESH).wait_recv()
    for c, e in sends:
        c.wait_send()
        e.wait_send()
    local.wait()
    local_en.wait()


def exchange(jacobian, local_energy, n):
    rows, slabs, cols = jacobian.shape
    width = cols // n
    en = local_energy.reshape(1, rows)
    return pl.pallas_call(
        functools.partial(exchange_kernel, n, width),
        out_shape=(
            jax.ShapeDtypeStruct((n, rows, slabs, width), jacobian.dtype),
            jax.ShapeDtypeStruct((n, 1, rows), local_energy.dtype),
        ),
        in_specs=[pl.BlockSpec(memory_space=pl.ANY)] * 2,
        out_specs=(pl.BlockSpec(memory_space=pl.ANY), pl.BlockSpec(memory_space=pl.ANY)),
        scratch_shapes=[
            pltpu.SemaphoreType.DMA((n,)),
            pltpu.SemaphoreType.DMA((n,)),
            pltpu.SemaphoreType.DMA((n,)),
            pltpu.SemaphoreType.DMA((n,)),
            pltpu.SemaphoreType.DMA((2,)),
        ],
        compiler_params=pltpu.CompilerParams(has_side_effects=True),
    )(jacobian, en)


def shards(n, jacobian, local_energy):
    gathered, energies = exchange(jacobian, local_energy, n)
    energies = energies.reshape(-1)
    samples = energies.shape[0]
    root_count = jnp.sqrt(jnp.float32(samples))
    eps = (energies - jnp.mean(energies)) / root_count
    columns = gathered.reshape(samples, gathered.shape[2], gathered.shape[3])
    slab_count = columns.shape[1]
    width = columns.shape[2]
    values = columns.astype(jnp.float32)
    mean_row = jnp.mean(values, axis=0, keepdims=True)
    centered = (
        ((values - mean_row) / root_count).astype(jnp.bfloat16).reshape(samples, slab_count * width)
    )
    partial_gram = jnp.dot(centered, centered.T, preferred_element_type=jnp.float32)
    gram = lax.psum(lax.psum(lax.psum(partial_gram, "col"), "slab"), "smp")
    shift = 0.01 * jnp.trace(gram) / samples
    factor = jnp.linalg.cholesky(gram + shift * jnp.eye(samples, dtype=jnp.float32))
    middle = lax.linalg.triangular_solve(factor, eps[:, None], left_side=True, lower=True)
    coeffs = lax.linalg.triangular_solve(
        factor, middle, left_side=True, lower=True, transpose_a=True
    )[:, 0]
    delta = jnp.dot(coeffs, centered.astype(jnp.float32), precision=lax.Precision.HIGHEST)
    squared = jnp.dot(coeffs, jnp.dot(gram, coeffs, precision=lax.Precision.HIGHEST),
                      precision=lax.Precision.HIGHEST)
    limit = 0.3 * jnp.sqrt(jnp.float32(SLABS * SLAB_COLS))
    scaled = -jnp.minimum(1.0, limit / jnp.sqrt(squared)) * delta
    return scaled.reshape(slab_count, width)


def solution(mesh):
    in_specs = (P("smp", "slab", "col"), P("smp"))
    out_specs = P("slab", ("col", "smp"))
    return jax.shard_map(functools.partial(shards, mesh.shape["smp"]), mesh=mesh,
                         in_specs=in_specs, out_specs=out_specs, check_vma=False)
```

```python
import functools

import jax
import jax.numpy as jnp
from jax import lax
from jax.experimental import pallas as pl
from jax.experimental.pallas import tpu as pltpu
from jax.sharding import PartitionSpec as P

SLABS = 32
SLAB_COLS = 16384


def solve_kernel(block, l_ref, dinv_ref, b_ref, c_ref, y_ref, r_ref):
    n = l_ref.shape[0]
    nb = n // block
    lane = lax.broadcasted_iota(jnp.int32, (1, block), 1)
    hi = lax.Precision.HIGHEST
    for q in range(nb):
        lo = q * block
        r_q = b_ref[:, lo:lo + block]
        if q > 0:
            prev = jnp.broadcast_to(y_ref[:, :lo], (8, lo))
            r_q = r_q - lax.dot_general(prev, l_ref[lo:lo + block, :lo], (((1,), (1,)), ((), ())),
                                        precision=hi, preferred_element_type=jnp.float32)[0:1]

        def fwd(g, y_q, lo=lo, r_q=r_q):
            tile = l_ref[pl.ds(pl.multiple_of(lo + g * 8, 8), 8), lo:lo + block]
            for r in range(8):
                ii = g * 8 + r
                row = jnp.where(lane < ii, tile[r:r + 1, :], 0.0)
                ri = jnp.sum(jnp.where(lane == ii, r_q, 0.0), axis=1, keepdims=True)
                s = jnp.sum(row * y_q, axis=1, keepdims=True)
                yi = (ri - s) * dinv_ref[lo + ii]
                y_q = jnp.where(lane == ii, yi, y_q)
            return y_q

        y_ref[:, lo:lo + block] = lax.fori_loop(0, block // 8, fwd, jnp.zeros((1, block), jnp.float32))
    r_ref[...] = y_ref[...]
    for q in reversed(range(nb)):
        lo = q * block

        def bwd(k, carry, lo=lo):
            r_q, c_q = carry
            g = block // 8 - 1 - k
            tile = l_ref[pl.ds(pl.multiple_of(lo + g * 8, 8), 8), lo:lo + block]
            for r in reversed(range(8)):
                jj = g * 8 + r
                rj = jnp.sum(jnp.where(lane == jj, r_q, 0.0), axis=1, keepdims=True)
                cj = rj * dinv_ref[lo + jj]
                row = jnp.where(lane < jj, tile[r:r + 1, :], 0.0)
                r_q = r_q - cj * row
                c_q = jnp.where(lane == jj, cj, c_q)
            return r_q, c_q

        r_q = r_ref[:, lo:lo + block]
        _, c_q = lax.fori_loop(0, block // 8, bwd, (r_q, jnp.zeros((1, block), jnp.float32)))
        c_ref[:, lo:lo + block] = c_q
        if q > 0:
            cb = jnp.broadcast_to(c_q, (8, block))
            r_ref[:, :lo] = r_ref[:, :lo] - jnp.dot(
                cb, l_ref[lo:lo + block, :lo], precision=hi, preferred_element_type=jnp.float32)[0:1]


def cho_solve(factor, rhs, block=128):
    n = factor.shape[0]
    dinv = 1.0 / jnp.diagonal(factor)
    out = pl.pallas_call(
        functools.partial(solve_kernel, block),
        out_shape=jax.ShapeDtypeStruct((1, n), jnp.float32),
        in_specs=[pl.BlockSpec(memory_space=pltpu.VMEM),
                  pl.BlockSpec(memory_space=pltpu.SMEM),
                  pl.BlockSpec(memory_space=pltpu.VMEM)],
        out_specs=pl.BlockSpec(memory_space=pltpu.VMEM),
        scratch_shapes=[pltpu.VMEM((1, n), jnp.float32), pltpu.VMEM((1, n), jnp.float32)],
    )(factor, dinv, rhs.reshape(1, n))
    return out.reshape(n)


def exchange_kernel(n, width, jac_ref, en_ref, cols_ref, en_all_ref,
                    send_sems, recv_sems, en_send, en_recv, local_sems):
    me = lax.axis_index("smp")
    col = lax.axis_index("col")
    slab = lax.axis_index("slab")

    def piece(t):
        return jac_ref.at[:, :, pl.ds(pl.multiple_of(t * width, width), width)]

    local = pltpu.make_async_copy(piece(me), cols_ref.at[me], local_sems.at[0])
    local.start()
    local_en = pltpu.make_async_copy(en_ref, en_all_ref.at[me], local_sems.at[1])
    local_en.start()
    sends = []
    for k in range(1, n):
        t = lax.rem(me + k, n)
        dev = (t, col, slab)
        c = pltpu.make_async_remote_copy(
            src_ref=piece(t), dst_ref=cols_ref.at[me],
            send_sem=send_sems.at[t], recv_sem=recv_sems.at[me],
            device_id=dev, device_id_type=pl.DeviceIdType.MESH)
        c.start()
        e = pltpu.make_async_remote_copy(
            src_ref=en_ref, dst_ref=en_all_ref.at[me],
            send_sem=en_send.at[t], recv_sem=en_recv.at[me],
            device_id=dev, device_id_type=pl.DeviceIdType.MESH)
        e.start()
        sends.append((c, e))
    for k in range(1, n):
        s = lax.rem(me + n - k, n)
        dev = (s, col, slab)
        pltpu.make_async_remote_copy(
            src_ref=piece(me), dst_ref=cols_ref.at[s],
            send_sem=send_sems.at[s], recv_sem=recv_sems.at[s],
            device_id=dev, device_id_type=pl.DeviceIdType.MESH).wait_recv()
        pltpu.make_async_remote_copy(
            src_ref=en_ref, dst_ref=en_all_ref.at[s],
            send_sem=en_send.at[s], recv_sem=en_recv.at[s],
            device_id=dev, device_id_type=pl.DeviceIdType.MESH).wait_recv()
    for c, e in sends:
        c.wait_send()
        e.wait_send()
    local.wait()
    local_en.wait()


def exchange(jacobian, local_energy, n):
    rows, slabs, cols = jacobian.shape
    width = cols // n
    en = local_energy.reshape(1, rows)
    return pl.pallas_call(
        functools.partial(exchange_kernel, n, width),
        out_shape=(
            jax.ShapeDtypeStruct((n, rows, slabs, width), jacobian.dtype),
            jax.ShapeDtypeStruct((n, 1, rows), local_energy.dtype),
        ),
        in_specs=[pl.BlockSpec(memory_space=pl.ANY)] * 2,
        out_specs=(pl.BlockSpec(memory_space=pl.ANY), pl.BlockSpec(memory_space=pl.ANY)),
        scratch_shapes=[
            pltpu.SemaphoreType.DMA((n,)),
            pltpu.SemaphoreType.DMA((n,)),
            pltpu.SemaphoreType.DMA((n,)),
            pltpu.SemaphoreType.DMA((n,)),
            pltpu.SemaphoreType.DMA((2,)),
        ],
        compiler_params=pltpu.CompilerParams(has_side_effects=True),
    )(jacobian, en)


def shards(n, jacobian, local_energy):
    gathered, energies = exchange(jacobian, local_energy, n)
    energies = energies.reshape(-1)
    samples = energies.shape[0]
    root_count = jnp.sqrt(jnp.float32(samples))
    eps = (energies - jnp.mean(energies)) / root_count
    columns = gathered.reshape(samples, gathered.shape[2], gathered.shape[3])
    slab_count = columns.shape[1]
    width = columns.shape[2]
    values = columns.astype(jnp.float32)
    mean_row = jnp.mean(values, axis=0, keepdims=True)
    centered = (
        ((values - mean_row) / root_count).astype(jnp.bfloat16).reshape(samples, slab_count * width)
    )
    partial_gram = jnp.dot(centered, centered.T, preferred_element_type=jnp.float32)
    gram = lax.psum(partial_gram, ("smp", "col", "slab"))
    shift = 0.01 * jnp.trace(gram) / samples
    factor = jnp.linalg.cholesky(gram + shift * jnp.eye(samples, dtype=jnp.float32))
    coeffs = cho_solve(factor, eps)
    delta = jnp.dot(coeffs, centered.astype(jnp.float32), precision=lax.Precision.HIGHEST)
    squared = jnp.dot(coeffs, jnp.dot(gram, coeffs, precision=lax.Precision.HIGHEST),
                      precision=lax.Precision.HIGHEST)
    limit = 0.3 * jnp.sqrt(jnp.float32(SLABS * SLAB_COLS))
    scaled = -jnp.minimum(1.0, limit / jnp.sqrt(squared)) * delta
    return scaled.reshape(slab_count, width)


def solution(mesh):
    in_specs = (P("smp", "slab", "col"), P("smp"))
    out_specs = P("slab", ("col", "smp"))
    return jax.shard_map(functools.partial(shards, mesh.shape["smp"]), mesh=mesh,
                         in_specs=in_specs, out_specs=out_specs, check_vma=False)
```

```python
import functools

import jax
import jax.numpy as jnp
from jax import lax
from jax.experimental import pallas as pl
from jax.experimental.pallas import tpu as pltpu
from jax.sharding import PartitionSpec as P

SLABS = 32
SLAB_COLS = 16384


def exchange_kernel(n, width, jac_ref, en_ref, cols_ref, en_all_ref,
                    send_sems, recv_sems, en_send, en_recv, local_sems):
    me = lax.axis_index("smp")
    col = lax.axis_index("col")
    slab = lax.axis_index("slab")

    def piece(t):
        return jac_ref.at[:, :, pl.ds(pl.multiple_of(t * width, width), width)]

    local = pltpu.make_async_copy(piece(me), cols_ref.at[me], local_sems.at[0])
    local.start()
    local_en = pltpu.make_async_copy(en_ref, en_all_ref.at[me], local_sems.at[1])
    local_en.start()
    sends = []
    for k in range(1, n):
        t = jnp.bitwise_xor(me, jnp.where(col == 0, k, n - k))
        dev = (t, col, slab)
        c = pltpu.make_async_remote_copy(
            src_ref=piece(t), dst_ref=cols_ref.at[me],
            send_sem=send_sems.at[t], recv_sem=recv_sems.at[me],
            device_id=dev, device_id_type=pl.DeviceIdType.MESH)
        c.start()
        e = pltpu.make_async_remote_copy(
            src_ref=en_ref, dst_ref=en_all_ref.at[me],
            send_sem=en_send.at[t], recv_sem=en_recv.at[me],
            device_id=dev, device_id_type=pl.DeviceIdType.MESH)
        e.start()
        sends.append((c, e))
    for k in range(1, n):
        s = jnp.bitwise_xor(me, k)
        dev = (s, col, slab)
        pltpu.make_async_remote_copy(
            src_ref=piece(me), dst_ref=cols_ref.at[s],
            send_sem=send_sems.at[s], recv_sem=recv_sems.at[s],
            device_id=dev, device_id_type=pl.DeviceIdType.MESH).wait_recv()
        pltpu.make_async_remote_copy(
            src_ref=en_ref, dst_ref=en_all_ref.at[s],
            send_sem=en_send.at[s], recv_sem=en_recv.at[s],
            device_id=dev, device_id_type=pl.DeviceIdType.MESH).wait_recv()
    for c, e in sends:
        c.wait_send()
        e.wait_send()
    local.wait()
    local_en.wait()


def exchange(jacobian, local_energy, n):
    rows, slabs, cols = jacobian.shape
    width = cols // n
    en = local_energy.reshape(1, rows)
    return pl.pallas_call(
        functools.partial(exchange_kernel, n, width),
        out_shape=(
            jax.ShapeDtypeStruct((n, rows, slabs, width), jacobian.dtype),
            jax.ShapeDtypeStruct((n, 1, rows), local_energy.dtype),
        ),
        in_specs=[pl.BlockSpec(memory_space=pl.ANY)] * 2,
        out_specs=(pl.BlockSpec(memory_space=pl.ANY), pl.BlockSpec(memory_space=pl.ANY)),
        scratch_shapes=[
            pltpu.SemaphoreType.DMA((n,)),
            pltpu.SemaphoreType.DMA((n,)),
            pltpu.SemaphoreType.DMA((n,)),
            pltpu.SemaphoreType.DMA((n,)),
            pltpu.SemaphoreType.DMA((2,)),
        ],
        compiler_params=pltpu.CompilerParams(has_side_effects=True),
    )(jacobian, en)


def shards(n, jacobian, local_energy):
    gathered, energies = exchange(jacobian, local_energy, n)
    energies = energies.reshape(-1)
    samples = energies.shape[0]
    root_count = jnp.sqrt(jnp.float32(samples))
    eps = (energies - jnp.mean(energies)) / root_count
    columns = gathered.reshape(samples, gathered.shape[2], gathered.shape[3])
    slab_count = columns.shape[1]
    width = columns.shape[2]
    values = columns.astype(jnp.float32)
    mean_row = jnp.mean(values, axis=0, keepdims=True)
    centered = (
        ((values - mean_row) / root_count).astype(jnp.bfloat16).reshape(samples, slab_count * width)
    )
    partial_gram = jnp.dot(centered, centered.T, preferred_element_type=jnp.float32)
    gram = lax.psum(partial_gram, ("smp", "col", "slab"))
    shift = 0.01 * jnp.trace(gram) / samples
    factor = jnp.linalg.cholesky(gram + shift * jnp.eye(samples, dtype=jnp.float32))
    middle = lax.linalg.triangular_solve(factor, eps[:, None], left_side=True, lower=True)
    coeffs = lax.linalg.triangular_solve(
        factor, middle, left_side=True, lower=True, transpose_a=True
    )[:, 0]
    delta = jnp.dot(coeffs, centered.astype(jnp.float32), precision=lax.Precision.HIGHEST)
    squared = jnp.dot(coeffs, jnp.dot(gram, coeffs, precision=lax.Precision.HIGHEST),
                      precision=lax.Precision.HIGHEST)
    limit = 0.3 * jnp.sqrt(jnp.float32(SLABS * SLAB_COLS))
    scaled = -jnp.minimum(1.0, limit / jnp.sqrt(squared)) * delta
    return scaled.reshape(slab_count, width)


def solution(mesh):
    in_specs = (P("smp", "slab", "col"), P("smp"))
    out_specs = P("slab", ("col", "smp"))
    return jax.shard_map(functools.partial(shards, mesh.shape["smp"]), mesh=mesh,
                         in_specs=in_specs, out_specs=out_specs, check_vma=False)
```

```python
import functools

import jax
import jax.numpy as jnp
from jax import lax
from jax.experimental import pallas as pl
from jax.experimental.pallas import tpu as pltpu
from jax.sharding import PartitionSpec as P

SLABS = 32
SLAB_COLS = 16384


def exchange_kernel(n, width, jac_ref, en_ref, cols_ref, en_all_ref,
                    send_sems, recv_sems, en_send, en_recv, local_sems):
    me = lax.axis_index("smp")
    col = lax.axis_index("col")
    slab = lax.axis_index("slab")

    def piece(t):
        return jac_ref.at[:, :, pl.ds(pl.multiple_of(t * width, width), width)]

    barrier = pltpu.get_barrier_semaphore()
    for k in range(1, n):
        pl.semaphore_signal(barrier, inc=1, device_id=(jnp.bitwise_xor(me, k), col, slab),
                            device_id_type=pl.DeviceIdType.MESH)
    pl.semaphore_wait(barrier, n - 1)
    local = pltpu.make_async_copy(piece(me), cols_ref.at[me], local_sems.at[0])
    local.start()
    local_en = pltpu.make_async_copy(en_ref, en_all_ref.at[me], local_sems.at[1])
    local_en.start()
    sends = []
    for k in range(1, n):
        t = jnp.bitwise_xor(me, jnp.where(col == 0, k, n - k))
        dev = (t, col, slab)
        c = pltpu.make_async_remote_copy(
            src_ref=piece(t), dst_ref=cols_ref.at[me],
            send_sem=send_sems.at[t], recv_sem=recv_sems.at[me],
            device_id=dev, device_id_type=pl.DeviceIdType.MESH)
        c.start()
        e = pltpu.make_async_remote_copy(
            src_ref=en_ref, dst_ref=en_all_ref.at[me],
            send_sem=en_send.at[t], recv_sem=en_recv.at[me],
            device_id=dev, device_id_type=pl.DeviceIdType.MESH)
        e.start()
        sends.append((c, e))
    for k in range(1, n):
        s = jnp.bitwise_xor(me, k)
        dev = (s, col, slab)
        pltpu.make_async_remote_copy(
            src_ref=piece(me), dst_ref=cols_ref.at[s],
            send_sem=send_sems.at[s], recv_sem=recv_sems.at[s],
            device_id=dev, device_id_type=pl.DeviceIdType.MESH).wait_recv()
        pltpu.make_async_remote_copy(
            src_ref=en_ref, dst_ref=en_all_ref.at[s],
            send_sem=en_send.at[s], recv_sem=en_recv.at[s],
            device_id=dev, device_id_type=pl.DeviceIdType.MESH).wait_recv()
    for c, e in sends:
        c.wait_send()
        e.wait_send()
    local.wait()
    local_en.wait()


def exchange(jacobian, local_energy, n):
    rows, slabs, cols = jacobian.shape
    width = cols // n
    en = local_energy.reshape(1, rows)
    return pl.pallas_call(
        functools.partial(exchange_kernel, n, width),
        out_shape=(
            jax.ShapeDtypeStruct((n, rows, slabs, width), jacobian.dtype),
            jax.ShapeDtypeStruct((n, 1, rows), local_energy.dtype),
        ),
        in_specs=[pl.BlockSpec(memory_space=pl.ANY)] * 2,
        out_specs=(pl.BlockSpec(memory_space=pl.ANY), pl.BlockSpec(memory_space=pl.ANY)),
        scratch_shapes=[
            pltpu.SemaphoreType.DMA((n,)),
            pltpu.SemaphoreType.DMA((n,)),
            pltpu.SemaphoreType.DMA((n,)),
            pltpu.SemaphoreType.DMA((n,)),
            pltpu.SemaphoreType.DMA((2,)),
        ],
        compiler_params=pltpu.CompilerParams(collective_id=0, has_side_effects=True),
    )(jacobian, en)


def shards(n, jacobian, local_energy):
    gathered, energies = exchange(jacobian, local_energy, n)
    energies = energies.reshape(-1)
    samples = energies.shape[0]
    root_count = jnp.sqrt(jnp.float32(samples))
    eps = (energies - jnp.mean(energies)) / root_count
    columns = gathered.reshape(samples, gathered.shape[2], gathered.shape[3])
    slab_count = columns.shape[1]
    width = columns.shape[2]
    values = columns.astype(jnp.float32)
    mean_row = jnp.mean(values, axis=0, keepdims=True)
    centered = (
        ((values - mean_row) / root_count).astype(jnp.bfloat16).reshape(samples, slab_count * width)
    )
    partial_gram = jnp.dot(centered, centered.T, preferred_element_type=jnp.float32)
    gram = lax.psum(partial_gram, ("smp", "col", "slab"))
    shift = 0.01 * jnp.trace(gram) / samples
    factor = lax.linalg.cholesky(gram + shift * jnp.eye(samples, dtype=jnp.float32),
                                 symmetrize_input=False)
    middle = lax.linalg.triangular_solve(factor, eps[:, None], left_side=True, lower=True)
    coeffs = lax.linalg.triangular_solve(
        factor, middle, left_side=True, lower=True, transpose_a=True
    )[:, 0]
    delta = jnp.dot(coeffs, centered.astype(jnp.float32), precision=lax.Precision.HIGHEST)
    squared = jnp.dot(coeffs, jnp.dot(gram, coeffs, precision=lax.Precision.HIGHEST),
                      precision=lax.Precision.HIGHEST)
    limit = 0.3 * jnp.sqrt(jnp.float32(SLABS * SLAB_COLS))
    scaled = -jnp.minimum(1.0, limit / jnp.sqrt(squared)) * delta
    return scaled.reshape(slab_count, width)


def solution(mesh):
    in_specs = (P("smp", "slab", "col"), P("smp"))
    out_specs = P("slab", ("col", "smp"))
    return jax.shard_map(functools.partial(shards, mesh.shape["smp"]), mesh=mesh,
                         in_specs=in_specs, out_specs=out_specs, check_vma=False)
```

```python
import functools

import jax
import jax.numpy as jnp
from jax import lax
from jax.experimental import pallas as pl
from jax.experimental.pallas import tpu as pltpu
from jax.sharding import PartitionSpec as P

SLABS = 32
SLAB_COLS = 16384


def exchange_kernel(n, width, jac_ref, en_ref, cols_ref, en_all_ref,
                    send_sems, recv_sems, en_send, en_recv, local_sems):
    me = lax.axis_index("smp")
    col = lax.axis_index("col")
    slab = lax.axis_index("slab")

    def piece(t):
        return jac_ref.at[:, :, pl.ds(pl.multiple_of(t * width, width), width)]

    barrier = pltpu.get_barrier_semaphore()
    for k in range(1, n):
        pl.semaphore_signal(barrier, inc=1, device_id=(jnp.bitwise_xor(me, k), col, slab),
                            device_id_type=pl.DeviceIdType.MESH)
    pl.semaphore_wait(barrier, n - 1)
    local = pltpu.make_async_copy(piece(me), cols_ref.at[me], local_sems.at[0])
    local.start()
    local_en = pltpu.make_async_copy(en_ref, en_all_ref.at[me], local_sems.at[1])
    local_en.start()
    sends = []
    for k in range(1, n):
        t = jnp.bitwise_xor(me, jnp.where(col == 0, k, n - k))
        dev = (t, col, slab)
        c = pltpu.make_async_remote_copy(
            src_ref=piece(t), dst_ref=cols_ref.at[me],
            send_sem=send_sems.at[t], recv_sem=recv_sems.at[me],
            device_id=dev, device_id_type=pl.DeviceIdType.MESH)
        c.start()
        e = pltpu.make_async_remote_copy(
            src_ref=en_ref, dst_ref=en_all_ref.at[me],
            send_sem=en_send.at[t], recv_sem=en_recv.at[me],
            device_id=dev, device_id_type=pl.DeviceIdType.MESH)
        e.start()
        sends.append((c, e))
    for k in range(1, n):
        s = jnp.bitwise_xor(me, k)
        dev = (s, col, slab)
        pltpu.make_async_remote_copy(
            src_ref=piece(me), dst_ref=cols_ref.at[s],
            send_sem=send_sems.at[s], recv_sem=recv_sems.at[s],
            device_id=dev, device_id_type=pl.DeviceIdType.MESH).wait_recv()
        pltpu.make_async_remote_copy(
            src_ref=en_ref, dst_ref=en_all_ref.at[s],
            send_sem=en_send.at[s], recv_sem=en_recv.at[s],
            device_id=dev, device_id_type=pl.DeviceIdType.MESH).wait_recv()
    for c, e in sends:
        c.wait_send()
        e.wait_send()
    local.wait()
    local_en.wait()


def exchange(jacobian, local_energy, n):
    rows, slabs, cols = jacobian.shape
    width = cols // n
    en = local_energy.reshape(1, rows)
    return pl.pallas_call(
        functools.partial(exchange_kernel, n, width),
        out_shape=(
            jax.ShapeDtypeStruct((n, rows, slabs, width), jacobian.dtype),
            jax.ShapeDtypeStruct((n, 1, rows), local_energy.dtype),
        ),
        in_specs=[pl.BlockSpec(memory_space=pl.ANY)] * 2,
        out_specs=(pl.BlockSpec(memory_space=pl.ANY), pl.BlockSpec(memory_space=pl.ANY)),
        scratch_shapes=[
            pltpu.SemaphoreType.DMA((n,)),
            pltpu.SemaphoreType.DMA((n,)),
            pltpu.SemaphoreType.DMA((n,)),
            pltpu.SemaphoreType.DMA((n,)),
            pltpu.SemaphoreType.DMA((2,)),
        ],
        compiler_params=pltpu.CompilerParams(collective_id=0, has_side_effects=True),
    )(jacobian, en)


def reduce_kernel(n, parts, p_ref, out_ref, rs_buf, ar_buf, acc_ref, rs_send, rs_recv,
                  ar_send, ar_recv, ag_send, ag_recv, local_sem):
    me = lax.axis_index("smp")
    col = lax.axis_index("col")
    slab = lax.axis_index("slab")
    cs = col * 2 + slab
    mesh_id = pl.DeviceIdType.MESH

    def peer(k):
        return jnp.bitwise_xor(me, jnp.where(col == 0, k, n - k))

    barrier = pltpu.get_barrier_semaphore()
    for k in range(1, n):
        pl.semaphore_signal(barrier, inc=1, device_id=(jnp.bitwise_xor(me, k), col, slab),
                            device_id_type=mesh_id)
    for k in range(1, parts):
        other = jnp.bitwise_xor(cs, k)
        pl.semaphore_signal(barrier, inc=1, device_id=(me, other // 2, other % 2),
                            device_id_type=mesh_id)
    pl.semaphore_wait(barrier, n - 1 + parts - 1)

    sends = []
    for k in range(1, n):
        t = peer(k)
        c = pltpu.make_async_remote_copy(
            src_ref=p_ref.at[t], dst_ref=rs_buf.at[me], send_sem=rs_send.at[t],
            recv_sem=rs_recv.at[me], device_id=(t, col, slab), device_id_type=mesh_id)
        c.start()
        sends.append(c)
    rs_buf[pl.ds(me, 1)] = p_ref[pl.ds(me, 1)]
    for k in range(1, n):
        s = jnp.bitwise_xor(me, k)
        pltpu.make_async_remote_copy(
            src_ref=p_ref.at[s], dst_ref=rs_buf.at[s], send_sem=rs_send.at[s],
            recv_sem=rs_recv.at[s], device_id=(s, col, slab), device_id_type=mesh_id).wait_recv()
    total = rs_buf[0]
    for s in range(1, n):
        total = total + rs_buf[s]
    ar_buf[pl.ds(cs, 1)] = total[None]
    for k in range(1, parts):
        other = jnp.bitwise_xor(cs, k)
        c = pltpu.make_async_remote_copy(
            src_ref=ar_buf.at[cs], dst_ref=ar_buf.at[cs], send_sem=ar_send.at[other],
            recv_sem=ar_recv.at[cs], device_id=(me, other // 2, other % 2), device_id_type=mesh_id)
        c.start()
        sends.append(c)
    for k in range(1, parts):
        other = jnp.bitwise_xor(cs, k)
        pltpu.make_async_remote_copy(
            src_ref=ar_buf.at[other], dst_ref=ar_buf.at[other], send_sem=ar_send.at[other],
            recv_sem=ar_recv.at[other], device_id=(me, other // 2, other % 2),
            device_id_type=mesh_id).wait_recv()
    total = ar_buf[0]
    for j in range(1, parts):
        total = total + ar_buf[j]
    acc_ref[...] = total
    local = pltpu.make_async_copy(acc_ref, out_ref.at[me], local_sem.at[0])
    local.start()
    for k in range(1, n):
        t = peer(k)
        c = pltpu.make_async_remote_copy(
            src_ref=acc_ref, dst_ref=out_ref.at[me], send_sem=ag_send.at[t],
            recv_sem=ag_recv.at[me], device_id=(t, col, slab), device_id_type=mesh_id)
        c.start()
        sends.append(c)
    for k in range(1, n):
        s = jnp.bitwise_xor(me, k)
        pltpu.make_async_remote_copy(
            src_ref=acc_ref, dst_ref=out_ref.at[s], send_sem=ag_send.at[s],
            recv_sem=ag_recv.at[s], device_id=(s, col, slab), device_id_type=mesh_id).wait_recv()
    for c in sends:
        c.wait_send()
    local.wait()


def lower_psum(partial, n, parts, block=128):
    size = partial.shape[0]
    nb = size // block
    pairs = [(i, j) for i in range(nb) for j in range(i + 1)]
    packed = jnp.concatenate(
        [partial[i * block:(i + 1) * block, j * block:(j + 1) * block] for i, j in pairs], axis=0)
    rows = packed.shape[0] // n
    packed = packed.reshape(n, rows, block)
    reduced = pl.pallas_call(
        functools.partial(reduce_kernel, n, parts),
        out_shape=jax.ShapeDtypeStruct((n, rows, block), jnp.float32),
        in_specs=[pl.BlockSpec(memory_space=pltpu.VMEM)],
        out_specs=pl.BlockSpec(memory_space=pl.ANY),
        scratch_shapes=[
            pltpu.VMEM((n, rows, block), jnp.float32),
            pltpu.VMEM((parts, rows, block), jnp.float32),
            pltpu.VMEM((rows, block), jnp.float32),
            pltpu.SemaphoreType.DMA((n,)),
            pltpu.SemaphoreType.DMA((n,)),
            pltpu.SemaphoreType.DMA((parts,)),
            pltpu.SemaphoreType.DMA((parts,)),
            pltpu.SemaphoreType.DMA((n,)),
            pltpu.SemaphoreType.DMA((n,)),
            pltpu.SemaphoreType.DMA((1,)),
        ],
        compiler_params=pltpu.CompilerParams(collective_id=1, has_side_effects=True),
    )(packed)
    blocks = reduced.reshape(len(pairs), block, block)
    where = {p: k for k, p in enumerate(pairs)}
    zero = jnp.zeros((block, block), jnp.float32)
    lower = jnp.concatenate([
        jnp.concatenate([blocks[where[(i, j)]] if j <= i else zero for j in range(nb)], axis=1)
        for i in range(nb)], axis=0)
    diag = jnp.stack([blocks[where[(i, i)]] for i in range(nb)])
    return lower, diag


def shards(n, jacobian, local_energy):
    gathered, energies = exchange(jacobian, local_energy, n)
    energies = energies.reshape(-1)
    samples = energies.shape[0]
    root_count = jnp.sqrt(jnp.float32(samples))
    eps = (energies - jnp.mean(energies)) / root_count
    columns = gathered.reshape(samples, gathered.shape[2], gathered.shape[3])
    slab_count = columns.shape[1]
    width = columns.shape[2]
    values = columns.astype(jnp.float32)
    mean_row = jnp.mean(values, axis=0, keepdims=True)
    centered = (
        ((values - mean_row) / root_count).astype(jnp.bfloat16).reshape(samples, slab_count * width)
    )
    partial_gram = jnp.dot(centered, centered.T, preferred_element_type=jnp.float32)
    parts = lax.psum(1, ("col", "slab"))
    gram, diag = lower_psum(partial_gram, n, parts)
    shift = 0.01 * jnp.trace(gram) / samples
    factor = lax.linalg.cholesky(gram + shift * jnp.eye(samples, dtype=jnp.float32),
                                 symmetrize_input=False)
    middle = lax.linalg.triangular_solve(factor, eps[:, None], left_side=True, lower=True)
    coeffs = lax.linalg.triangular_solve(
        factor, middle, left_side=True, lower=True, transpose_a=True
    )[:, 0]
    delta = jnp.dot(coeffs, centered.astype(jnp.float32), precision=lax.Precision.HIGHEST)
    hi = lax.Precision.HIGHEST
    blocked = coeffs.reshape(diag.shape[0], diag.shape[1])
    full_c = (jnp.dot(gram, coeffs, precision=hi) + jnp.dot(coeffs, gram, precision=hi)
              - jnp.einsum("bij,bj->bi", diag, blocked, precision=hi).reshape(-1))
    squared = jnp.dot(coeffs, full_c, precision=hi)
    limit = 0.3 * jnp.sqrt(jnp.float32(SLABS * SLAB_COLS))
    scaled = -jnp.minimum(1.0, limit / jnp.sqrt(squared)) * delta
    return scaled.reshape(slab_count, width)


def solution(mesh):
    in_specs = (P("smp", "slab", "col"), P("smp"))
    out_specs = P("slab", ("col", "smp"))
    return jax.shard_map(functools.partial(shards, mesh.shape["smp"]), mesh=mesh,
                         in_specs=in_specs, out_specs=out_specs, check_vma=False)
```

```python
import functools

import jax
import jax.numpy as jnp
from jax import lax
from jax.experimental import pallas as pl
from jax.experimental.pallas import tpu as pltpu
from jax.sharding import PartitionSpec as P

SLABS = 32
SLAB_COLS = 16384


def exchange_kernel(n, width, jac_ref, en_ref, cols_ref, en_all_ref,
                    send_sems, recv_sems, en_send, en_recv, local_sems):
    me = lax.axis_index("smp")
    col = lax.axis_index("col")
    slab = lax.axis_index("slab")

    def piece(t):
        return jac_ref.at[:, :, pl.ds(pl.multiple_of(t * width, width), width)]

    barrier = pltpu.get_barrier_semaphore()
    for k in range(1, n):
        pl.semaphore_signal(barrier, inc=1, device_id=(jnp.bitwise_xor(me, k), col, slab),
                            device_id_type=pl.DeviceIdType.MESH)
    pl.semaphore_wait(barrier, n - 1)
    local = pltpu.make_async_copy(piece(me), cols_ref.at[me], local_sems.at[0])
    local.start()
    local_en = pltpu.make_async_copy(en_ref, en_all_ref.at[me], local_sems.at[1])
    local_en.start()
    sends = []
    for k in range(1, n):
        t = jnp.bitwise_xor(me, jnp.where(col == 0, k, n - k))
        dev = (t, col, slab)
        c = pltpu.make_async_remote_copy(
            src_ref=piece(t), dst_ref=cols_ref.at[me],
            send_sem=send_sems.at[t], recv_sem=recv_sems.at[me],
            device_id=dev, device_id_type=pl.DeviceIdType.MESH)
        c.start()
        e = pltpu.make_async_remote_copy(
            src_ref=en_ref, dst_ref=en_all_ref.at[me],
            send_sem=en_send.at[t], recv_sem=en_recv.at[me],
            device_id=dev, device_id_type=pl.DeviceIdType.MESH)
        e.start()
        sends.append((c, e))
    for k in range(1, n):
        s = jnp.bitwise_xor(me, k)
        dev = (s, col, slab)
        pltpu.make_async_remote_copy(
            src_ref=piece(me), dst_ref=cols_ref.at[s],
            send_sem=send_sems.at[s], recv_sem=recv_sems.at[s],
            device_id=dev, device_id_type=pl.DeviceIdType.MESH).wait_recv()
        pltpu.make_async_remote_copy(
            src_ref=en_ref, dst_ref=en_all_ref.at[s],
            send_sem=en_send.at[s], recv_sem=en_recv.at[s],
            device_id=dev, device_id_type=pl.DeviceIdType.MESH).wait_recv()
    for c, e in sends:
        c.wait_send()
        e.wait_send()
    local.wait()
    local_en.wait()


def exchange(jacobian, local_energy, n):
    rows, slabs, cols = jacobian.shape
    width = cols // n
    en = local_energy.reshape(1, rows)
    return pl.pallas_call(
        functools.partial(exchange_kernel, n, width),
        out_shape=(
            jax.ShapeDtypeStruct((n, rows, slabs, width), jacobian.dtype),
            jax.ShapeDtypeStruct((n, 1, rows), local_energy.dtype),
        ),
        in_specs=[pl.BlockSpec(memory_space=pl.ANY)] * 2,
        out_specs=(pl.BlockSpec(memory_space=pl.ANY), pl.BlockSpec(memory_space=pl.ANY)),
        scratch_shapes=[
            pltpu.SemaphoreType.DMA((n,)),
            pltpu.SemaphoreType.DMA((n,)),
            pltpu.SemaphoreType.DMA((n,)),
            pltpu.SemaphoreType.DMA((n,)),
            pltpu.SemaphoreType.DMA((2,)),
        ],
        compiler_params=pltpu.CompilerParams(collective_id=0, has_side_effects=True),
    )(jacobian, en)


def reduce_kernel(n, parts, p_ref, out_ref, rs_buf, ar_buf, acc_ref, rs_send, rs_recv,
                  ar_send, ar_recv, ag_send, ag_recv, local_sem):
    me = lax.axis_index("smp")
    col = lax.axis_index("col")
    slab = lax.axis_index("slab")
    cs = col * 2 + slab
    mesh_id = pl.DeviceIdType.MESH

    def peer(k):
        return jnp.bitwise_xor(me, jnp.where(col == 0, k, n - k))

    barrier = pltpu.get_barrier_semaphore()
    for k in range(1, n):
        pl.semaphore_signal(barrier, inc=1, device_id=(jnp.bitwise_xor(me, k), col, slab),
                            device_id_type=mesh_id)
    for k in range(1, parts):
        other = jnp.bitwise_xor(cs, k)
        pl.semaphore_signal(barrier, inc=1, device_id=(me, other // 2, other % 2),
                            device_id_type=mesh_id)
    pl.semaphore_wait(barrier, n - 1 + parts - 1)

    sends = []
    for k in range(1, n):
        t = peer(k)
        c = pltpu.make_async_remote_copy(
            src_ref=p_ref.at[t], dst_ref=rs_buf.at[me], send_sem=rs_send.at[t],
            recv_sem=rs_recv.at[me], device_id=(t, col, slab), device_id_type=mesh_id)
        c.start()
        sends.append(c)
    rs_buf[pl.ds(me, 1)] = p_ref[pl.ds(me, 1)]
    for k in range(1, n):
        s = jnp.bitwise_xor(me, k)
        pltpu.make_async_remote_copy(
            src_ref=p_ref.at[s], dst_ref=rs_buf.at[s], send_sem=rs_send.at[s],
            recv_sem=rs_recv.at[s], device_id=(s, col, slab), device_id_type=mesh_id).wait_recv()
    total = rs_buf[0]
    for s in range(1, n):
        total = total + rs_buf[s]
    ar_buf[pl.ds(cs, 1)] = total[None]
    for k in range(1, parts):
        other = jnp.bitwise_xor(cs, k)
        c = pltpu.make_async_remote_copy(
            src_ref=ar_buf.at[cs], dst_ref=ar_buf.at[cs], send_sem=ar_send.at[other],
            recv_sem=ar_recv.at[cs], device_id=(me, other // 2, other % 2), device_id_type=mesh_id)
        c.start()
        sends.append(c)
    for k in range(1, parts):
        other = jnp.bitwise_xor(cs, k)
        pltpu.make_async_remote_copy(
            src_ref=ar_buf.at[other], dst_ref=ar_buf.at[other], send_sem=ar_send.at[other],
            recv_sem=ar_recv.at[other], device_id=(me, other // 2, other % 2),
            device_id_type=mesh_id).wait_recv()
    total = ar_buf[0]
    for j in range(1, parts):
        total = total + ar_buf[j]
    acc_ref[...] = total
    local = pltpu.make_async_copy(acc_ref, out_ref.at[me], local_sem.at[0])
    local.start()
    for k in range(1, n):
        t = peer(k)
        c = pltpu.make_async_remote_copy(
            src_ref=acc_ref, dst_ref=out_ref.at[me], send_sem=ag_send.at[t],
            recv_sem=ag_recv.at[me], device_id=(t, col, slab), device_id_type=mesh_id)
        c.start()
        sends.append(c)
    for k in range(1, n):
        s = jnp.bitwise_xor(me, k)
        pltpu.make_async_remote_copy(
            src_ref=acc_ref, dst_ref=out_ref.at[s], send_sem=ag_send.at[s],
            recv_sem=ag_recv.at[s], device_id=(s, col, slab), device_id_type=mesh_id).wait_recv()
    for c in sends:
        c.wait_send()
    local.wait()


def lower_psum(partial, n, parts, block=128):
    size = partial.shape[0]
    nb = size // block
    pairs = [(i, j) for i in range(nb) for j in range(i + 1)]
    packed = jnp.concatenate(
        [partial[i * block:(i + 1) * block, j * block:(j + 1) * block] for i, j in pairs], axis=0)
    rows = packed.shape[0] // n
    packed = packed.reshape(n, rows, block)
    reduced = pl.pallas_call(
        functools.partial(reduce_kernel, n, parts),
        out_shape=jax.ShapeDtypeStruct((n, rows, block), jnp.float32),
        in_specs=[pl.BlockSpec(memory_space=pltpu.VMEM)],
        out_specs=pl.BlockSpec(memory_space=pl.ANY),
        scratch_shapes=[
            pltpu.VMEM((n, rows, block), jnp.float32),
            pltpu.VMEM((parts, rows, block), jnp.float32),
            pltpu.VMEM((rows, block), jnp.float32),
            pltpu.SemaphoreType.DMA((n,)),
            pltpu.SemaphoreType.DMA((n,)),
            pltpu.SemaphoreType.DMA((parts,)),
            pltpu.SemaphoreType.DMA((parts,)),
            pltpu.SemaphoreType.DMA((n,)),
            pltpu.SemaphoreType.DMA((n,)),
            pltpu.SemaphoreType.DMA((1,)),
        ],
        compiler_params=pltpu.CompilerParams(collective_id=1, has_side_effects=True),
    )(packed)
    blocks = reduced.reshape(len(pairs), block, block)
    where = {p: k for k, p in enumerate(pairs)}
    zero = jnp.zeros((block, block), jnp.float32)
    lower = jnp.concatenate([
        jnp.concatenate([blocks[where[(i, j)]] if j <= i else zero for j in range(nb)], axis=1)
        for i in range(nb)], axis=0)
    diag = jnp.stack([blocks[where[(i, i)]] for i in range(nb)])
    return lower, diag


def cholesky_solve(a, rhs, block=128):
    n = a.shape[0]
    nb = n // block
    hi = lax.Precision.HIGHEST
    eye = jnp.eye(block, dtype=jnp.float32)
    inverses, panels, factors = [], [], []
    for k in range(nb):
        lo = k * block
        lkk = lax.linalg.cholesky(a[lo:lo + block, lo:lo + block], symmetrize_input=False)
        inv = lax.linalg.triangular_solve(lkk, eye, left_side=True, lower=True)
        factors.append(lkk)
        inverses.append(inv)
        if k < nb - 1:
            panel = jnp.dot(a[lo + block:, lo:lo + block], inv.T, precision=hi)
            panels.append(panel)
            a = a.at[lo + block:, lo + block:].add(-jnp.dot(panel, panel.T, precision=hi))
    ys = []
    for k in range(nb):
        lo = k * block
        r = rhs[lo:lo + block]
        if k > 0:
            strip = jnp.concatenate(
                [panels[j][(k - j - 1) * block:(k - j) * block] for j in range(k)], axis=1)
            r = r - jnp.dot(strip, jnp.concatenate(ys), precision=hi)
        ys.append(jnp.dot(inverses[k], r, precision=hi))
    cs = [None] * nb
    for k in reversed(range(nb)):
        r = ys[k]
        if k < nb - 1:
            r = r - jnp.dot(jnp.concatenate(cs[k + 1:]), panels[k], precision=hi)
        cs[k] = jnp.dot(r, inverses[k], precision=hi)
    return jnp.concatenate(cs)


def shards(n, jacobian, local_energy):
    gathered, energies = exchange(jacobian, local_energy, n)
    energies = energies.reshape(-1)
    samples = energies.shape[0]
    root_count = jnp.sqrt(jnp.float32(samples))
    eps = (energies - jnp.mean(energies)) / root_count
    columns = gathered.reshape(samples, gathered.shape[2], gathered.shape[3])
    slab_count = columns.shape[1]
    width = columns.shape[2]
    values = columns.astype(jnp.float32)
    mean_row = jnp.mean(values, axis=0, keepdims=True)
    centered = (
        ((values - mean_row) / root_count).astype(jnp.bfloat16).reshape(samples, slab_count * width)
    )
    partial_gram = jnp.dot(centered, centered.T, preferred_element_type=jnp.float32)
    parts = lax.psum(1, ("col", "slab"))
    gram, diag = lower_psum(partial_gram, n, parts)
    shift = 0.01 * jnp.trace(gram) / samples
    coeffs = cholesky_solve(gram + shift * jnp.eye(samples, dtype=jnp.float32), eps)
    delta = jnp.dot(coeffs, centered.astype(jnp.float32), precision=lax.Precision.HIGHEST)
    hi = lax.Precision.HIGHEST
    blocked = coeffs.reshape(diag.shape[0], diag.shape[1])
    full_c = (jnp.dot(gram, coeffs, precision=hi) + jnp.dot(coeffs, gram, precision=hi)
              - jnp.einsum("bij,bj->bi", diag, blocked, precision=hi).reshape(-1))
    squared = jnp.dot(coeffs, full_c, precision=hi)
    limit = 0.3 * jnp.sqrt(jnp.float32(SLABS * SLAB_COLS))
    scaled = -jnp.minimum(1.0, limit / jnp.sqrt(squared)) * delta
    return scaled.reshape(slab_count, width)


def solution(mesh):
    in_specs = (P("smp", "slab", "col"), P("smp"))
    out_specs = P("slab", ("col", "smp"))
    return jax.shard_map(functools.partial(shards, mesh.shape["smp"]), mesh=mesh,
                         in_specs=in_specs, out_specs=out_specs, check_vma=False)
```

```python
import functools

import jax
import jax.numpy as jnp
from jax import lax
from jax.experimental import pallas as pl
from jax.experimental.pallas import tpu as pltpu
from jax.sharding import PartitionSpec as P

SLABS = 32
SLAB_COLS = 16384


def exchange_kernel(n, width, jac_ref, en_ref, cols_ref, en_all_ref,
                    send_sems, recv_sems, en_send, en_recv, local_sems):
    me = lax.axis_index("smp")
    col = lax.axis_index("col")
    slab = lax.axis_index("slab")

    def piece(t):
        return jac_ref.at[:, :, pl.ds(pl.multiple_of(t * width, width), width)]

    barrier = pltpu.get_barrier_semaphore()
    for k in range(1, n):
        pl.semaphore_signal(barrier, inc=1, device_id=(jnp.bitwise_xor(me, k), col, slab),
                            device_id_type=pl.DeviceIdType.MESH)
    pl.semaphore_wait(barrier, n - 1)
    local = pltpu.make_async_copy(piece(me), cols_ref.at[me], local_sems.at[0])
    local.start()
    local_en = pltpu.make_async_copy(en_ref, en_all_ref.at[me], local_sems.at[1])
    local_en.start()
    sends = []
    for k in range(1, n):
        t = jnp.bitwise_xor(me, jnp.where(col == 0, k, n - k))
        dev = (t, col, slab)
        c = pltpu.make_async_remote_copy(
            src_ref=piece(t), dst_ref=cols_ref.at[me],
            send_sem=send_sems.at[t], recv_sem=recv_sems.at[me],
            device_id=dev, device_id_type=pl.DeviceIdType.MESH)
        c.start()
        e = pltpu.make_async_remote_copy(
            src_ref=en_ref, dst_ref=en_all_ref.at[me],
            send_sem=en_send.at[t], recv_sem=en_recv.at[me],
            device_id=dev, device_id_type=pl.DeviceIdType.MESH)
        e.start()
        sends.append((c, e))
    for k in range(1, n):
        s = jnp.bitwise_xor(me, k)
        dev = (s, col, slab)
        pltpu.make_async_remote_copy(
            src_ref=piece(me), dst_ref=cols_ref.at[s],
            send_sem=send_sems.at[s], recv_sem=recv_sems.at[s],
            device_id=dev, device_id_type=pl.DeviceIdType.MESH).wait_recv()
        pltpu.make_async_remote_copy(
            src_ref=en_ref, dst_ref=en_all_ref.at[s],
            send_sem=en_send.at[s], recv_sem=en_recv.at[s],
            device_id=dev, device_id_type=pl.DeviceIdType.MESH).wait_recv()
    for c, e in sends:
        c.wait_send()
        e.wait_send()
    local.wait()
    local_en.wait()


def exchange(jacobian, local_energy, n):
    rows, slabs, cols = jacobian.shape
    width = cols // n
    en = local_energy.reshape(1, rows)
    return pl.pallas_call(
        functools.partial(exchange_kernel, n, width),
        out_shape=(
            jax.ShapeDtypeStruct((n, rows, slabs, width), jacobian.dtype),
            jax.ShapeDtypeStruct((n, 1, rows), local_energy.dtype),
        ),
        in_specs=[pl.BlockSpec(memory_space=pl.ANY)] * 2,
        out_specs=(pl.BlockSpec(memory_space=pl.ANY), pl.BlockSpec(memory_space=pl.ANY)),
        scratch_shapes=[
            pltpu.SemaphoreType.DMA((n,)),
            pltpu.SemaphoreType.DMA((n,)),
            pltpu.SemaphoreType.DMA((n,)),
            pltpu.SemaphoreType.DMA((n,)),
            pltpu.SemaphoreType.DMA((2,)),
        ],
        compiler_params=pltpu.CompilerParams(collective_id=0, has_side_effects=True),
    )(jacobian, en)


def reduce_kernel(n, parts, p_ref, out_ref, rs_buf, ar_buf, acc_ref, rs_send, rs_recv,
                  ar_send, ar_recv, ag_send, ag_recv, local_sem):
    me = lax.axis_index("smp")
    col = lax.axis_index("col")
    slab = lax.axis_index("slab")
    cs = col * 2 + slab
    mesh_id = pl.DeviceIdType.MESH

    def peer(k):
        return jnp.bitwise_xor(me, jnp.where(col == 0, k, n - k))

    barrier = pltpu.get_barrier_semaphore()
    for k in range(1, n):
        pl.semaphore_signal(barrier, inc=1, device_id=(jnp.bitwise_xor(me, k), col, slab),
                            device_id_type=mesh_id)
    for k in range(1, parts):
        other = jnp.bitwise_xor(cs, k)
        pl.semaphore_signal(barrier, inc=1, device_id=(me, other // 2, other % 2),
                            device_id_type=mesh_id)
    pl.semaphore_wait(barrier, n - 1 + parts - 1)

    sends = []
    for k in range(1, n):
        t = peer(k)
        c = pltpu.make_async_remote_copy(
            src_ref=p_ref.at[t], dst_ref=rs_buf.at[me], send_sem=rs_send.at[t],
            recv_sem=rs_recv.at[me], device_id=(t, col, slab), device_id_type=mesh_id)
        c.start()
        sends.append(c)
    rs_buf[pl.ds(me, 1)] = p_ref[pl.ds(me, 1)]
    for k in range(1, n):
        s = jnp.bitwise_xor(me, k)
        pltpu.make_async_remote_copy(
            src_ref=p_ref.at[s], dst_ref=rs_buf.at[s], send_sem=rs_send.at[s],
            recv_sem=rs_recv.at[s], device_id=(s, col, slab), device_id_type=mesh_id).wait_recv()
    total = rs_buf[0]
    for s in range(1, n):
        total = total + rs_buf[s]
    ar_buf[pl.ds(cs, 1)] = total[None]
    for k in range(1, parts):
        other = jnp.bitwise_xor(cs, k)
        c = pltpu.make_async_remote_copy(
            src_ref=ar_buf.at[cs], dst_ref=ar_buf.at[cs], send_sem=ar_send.at[other],
            recv_sem=ar_recv.at[cs], device_id=(me, other // 2, other % 2), device_id_type=mesh_id)
        c.start()
        sends.append(c)
    for k in range(1, parts):
        other = jnp.bitwise_xor(cs, k)
        pltpu.make_async_remote_copy(
            src_ref=ar_buf.at[other], dst_ref=ar_buf.at[other], send_sem=ar_send.at[other],
            recv_sem=ar_recv.at[other], device_id=(me, other // 2, other % 2),
            device_id_type=mesh_id).wait_recv()
    total = ar_buf[0]
    for j in range(1, parts):
        total = total + ar_buf[j]
    acc_ref[...] = total
    local = pltpu.make_async_copy(acc_ref, out_ref.at[me], local_sem.at[0])
    local.start()
    for k in range(1, n):
        t = peer(k)
        c = pltpu.make_async_remote_copy(
            src_ref=acc_ref, dst_ref=out_ref.at[me], send_sem=ag_send.at[t],
            recv_sem=ag_recv.at[me], device_id=(t, col, slab), device_id_type=mesh_id)
        c.start()
        sends.append(c)
    for k in range(1, n):
        s = jnp.bitwise_xor(me, k)
        pltpu.make_async_remote_copy(
            src_ref=acc_ref, dst_ref=out_ref.at[s], send_sem=ag_send.at[s],
            recv_sem=ag_recv.at[s], device_id=(s, col, slab), device_id_type=mesh_id).wait_recv()
    for c in sends:
        c.wait_send()
    local.wait()


def lower_psum(partial, n, parts, block=128):
    size = partial.shape[0]
    nb = size // block
    pairs = [(i, j) for i in range(nb) for j in range(i + 1)]
    packed = jnp.concatenate(
        [partial[i * block:(i + 1) * block, j * block:(j + 1) * block] for i, j in pairs], axis=0)
    rows = packed.shape[0] // n
    packed = packed.reshape(n, rows, block)
    reduced = pl.pallas_call(
        functools.partial(reduce_kernel, n, parts),
        out_shape=jax.ShapeDtypeStruct((n, rows, block), jnp.float32),
        in_specs=[pl.BlockSpec(memory_space=pltpu.VMEM)],
        out_specs=pl.BlockSpec(memory_space=pl.ANY),
        scratch_shapes=[
            pltpu.VMEM((n, rows, block), jnp.float32),
            pltpu.VMEM((parts, rows, block), jnp.float32),
            pltpu.VMEM((rows, block), jnp.float32),
            pltpu.SemaphoreType.DMA((n,)),
            pltpu.SemaphoreType.DMA((n,)),
            pltpu.SemaphoreType.DMA((parts,)),
            pltpu.SemaphoreType.DMA((parts,)),
            pltpu.SemaphoreType.DMA((n,)),
            pltpu.SemaphoreType.DMA((n,)),
            pltpu.SemaphoreType.DMA((1,)),
        ],
        compiler_params=pltpu.CompilerParams(collective_id=1, has_side_effects=True),
    )(packed)
    blocks = reduced.reshape(len(pairs), block, block)
    where = {p: k for k, p in enumerate(pairs)}
    zero = jnp.zeros((block, block), jnp.float32)
    lower = jnp.concatenate([
        jnp.concatenate([blocks[where[(i, j)]] if j <= i else zero for j in range(nb)], axis=1)
        for i in range(nb)], axis=0)
    diag = jnp.stack([blocks[where[(i, i)]] for i in range(nb)])
    return lower, diag


def cholesky_solve(a, rhs, block=128):
    n = a.shape[0]
    nb = n // block
    hi = lax.Precision.HIGHEST
    eye = jnp.eye(block, dtype=jnp.float32)
    inverses, panels, factors = [], [], []
    for k in range(nb):
        lo = k * block
        lkk = lax.linalg.cholesky(a[lo:lo + block, lo:lo + block], symmetrize_input=False)
        inv = lax.linalg.triangular_solve(lkk, eye, left_side=True, lower=True)
        factors.append(lkk)
        inverses.append(inv)
        if k < nb - 1:
            panel = jnp.dot(a[lo + block:, lo:lo + block], inv.T, precision=hi)
            panels.append(panel)
            a = a.at[lo + block:, lo + block:].add(-jnp.dot(panel, panel.T, precision=hi))
    ys = []
    for k in range(nb):
        lo = k * block
        r = rhs[lo:lo + block]
        if k > 0:
            strip = jnp.concatenate(
                [panels[j][(k - j - 1) * block:(k - j) * block] for j in range(k)], axis=1)
            r = r - jnp.dot(strip, jnp.concatenate(ys), precision=hi)
        ys.append(jnp.dot(inverses[k], r, precision=hi))
    cs = [None] * nb
    for k in reversed(range(nb)):
        r = ys[k]
        if k < nb - 1:
            r = r - jnp.dot(jnp.concatenate(cs[k + 1:]), panels[k], precision=hi)
        cs[k] = jnp.dot(r, inverses[k], precision=hi)
    return jnp.concatenate(cs)


def shards(n, jacobian, local_energy):
    gathered, energies = exchange(jacobian, local_energy, n)
    energies = energies.reshape(-1)
    samples = energies.shape[0]
    root_count = jnp.sqrt(jnp.float32(samples))
    eps = (energies - jnp.mean(energies)) / root_count
    columns = gathered.reshape(samples, gathered.shape[2], gathered.shape[3])
    slab_count = columns.shape[1]
    width = columns.shape[2]
    values = columns.astype(jnp.float32)
    mean_row = jnp.mean(values, axis=0, keepdims=True)
    centered = (
        ((values - mean_row) / root_count).astype(jnp.bfloat16).reshape(samples, slab_count * width)
    )
    partial_gram = jnp.dot(centered, centered.T, preferred_element_type=jnp.float32)
    parts = lax.psum(1, ("col", "slab"))
    gram, diag = lower_psum(partial_gram, n, parts)
    shift = 0.01 * jnp.trace(gram) / samples
    coeffs = cholesky_solve(gram + shift * jnp.eye(samples, dtype=jnp.float32), eps)
    delta = jnp.sum(coeffs[:, None] * centered.astype(jnp.float32), axis=0)
    hi = lax.Precision.HIGHEST
    blocked = coeffs.reshape(diag.shape[0], diag.shape[1])
    full_c = (jnp.dot(gram, coeffs, precision=hi) + jnp.dot(coeffs, gram, precision=hi)
              - jnp.einsum("bij,bj->bi", diag, blocked, precision=hi).reshape(-1))
    squared = jnp.dot(coeffs, full_c, precision=hi)
    limit = 0.3 * jnp.sqrt(jnp.float32(SLABS * SLAB_COLS))
    scaled = -jnp.minimum(1.0, limit / jnp.sqrt(squared)) * delta
    return scaled.reshape(slab_count, width)


def solution(mesh):
    in_specs = (P("smp", "slab", "col"), P("smp"))
    out_specs = P("slab", ("col", "smp"))
    return jax.shard_map(functools.partial(shards, mesh.shape["smp"]), mesh=mesh,
                         in_specs=in_specs, out_specs=out_specs, check_vma=False)
```

```python
import functools

import jax
import jax.numpy as jnp
from jax import lax
from jax.experimental import pallas as pl
from jax.experimental.pallas import tpu as pltpu
from jax.sharding import PartitionSpec as P

SLABS = 32
SLAB_COLS = 16384


def exchange_kernel(n, width, jac_ref, en_ref, cols_ref, en_all_ref,
                    send_sems, recv_sems, en_send, en_recv, local_sems):
    me = lax.axis_index("smp")
    col = lax.axis_index("col")
    slab = lax.axis_index("slab")

    def piece(t):
        return jac_ref.at[:, :, pl.ds(pl.multiple_of(t * width, width), width)]

    barrier = pltpu.get_barrier_semaphore()
    for k in range(1, n):
        pl.semaphore_signal(barrier, inc=1, device_id=(jnp.bitwise_xor(me, k), col, slab),
                            device_id_type=pl.DeviceIdType.MESH)
    pl.semaphore_wait(barrier, n - 1)
    local = pltpu.make_async_copy(piece(me), cols_ref.at[me], local_sems.at[0])
    local.start()
    local_en = pltpu.make_async_copy(en_ref, en_all_ref.at[me], local_sems.at[1])
    local_en.start()
    sends = []
    for k in range(1, n):
        t = jnp.bitwise_xor(me, jnp.where(col == 0, k, n - k))
        dev = (t, col, slab)
        c = pltpu.make_async_remote_copy(
            src_ref=piece(t), dst_ref=cols_ref.at[me],
            send_sem=send_sems.at[t], recv_sem=recv_sems.at[me],
            device_id=dev, device_id_type=pl.DeviceIdType.MESH)
        c.start()
        e = pltpu.make_async_remote_copy(
            src_ref=en_ref, dst_ref=en_all_ref.at[me],
            send_sem=en_send.at[t], recv_sem=en_recv.at[me],
            device_id=dev, device_id_type=pl.DeviceIdType.MESH)
        e.start()
        sends.append((c, e))
    for k in range(1, n):
        s = jnp.bitwise_xor(me, k)
        dev = (s, col, slab)
        pltpu.make_async_remote_copy(
            src_ref=piece(me), dst_ref=cols_ref.at[s],
            send_sem=send_sems.at[s], recv_sem=recv_sems.at[s],
            device_id=dev, device_id_type=pl.DeviceIdType.MESH).wait_recv()
        pltpu.make_async_remote_copy(
            src_ref=en_ref, dst_ref=en_all_ref.at[s],
            send_sem=en_send.at[s], recv_sem=en_recv.at[s],
            device_id=dev, device_id_type=pl.DeviceIdType.MESH).wait_recv()
    for c, e in sends:
        c.wait_send()
        e.wait_send()
    local.wait()
    local_en.wait()


def exchange(jacobian, local_energy, n):
    rows, slabs, cols = jacobian.shape
    width = cols // n
    en = local_energy.reshape(1, rows)
    return pl.pallas_call(
        functools.partial(exchange_kernel, n, width),
        out_shape=(
            jax.ShapeDtypeStruct((n, rows, slabs, width), jacobian.dtype),
            jax.ShapeDtypeStruct((n, 1, rows), local_energy.dtype),
        ),
        in_specs=[pl.BlockSpec(memory_space=pl.ANY)] * 2,
        out_specs=(pl.BlockSpec(memory_space=pl.ANY), pl.BlockSpec(memory_space=pl.ANY)),
        scratch_shapes=[
            pltpu.SemaphoreType.DMA((n,)),
            pltpu.SemaphoreType.DMA((n,)),
            pltpu.SemaphoreType.DMA((n,)),
            pltpu.SemaphoreType.DMA((n,)),
            pltpu.SemaphoreType.DMA((2,)),
        ],
        compiler_params=pltpu.CompilerParams(collective_id=0, has_side_effects=True),
    )(jacobian, en)


def reduce_kernel(n, parts, p_ref, out_ref, rs_buf, ar_buf, acc_ref, rs_send, rs_recv,
                  ar_send, ar_recv, ag_send, ag_recv, local_sem):
    me = lax.axis_index("smp")
    col = lax.axis_index("col")
    slab = lax.axis_index("slab")
    cs = col * 2 + slab
    mesh_id = pl.DeviceIdType.MESH

    def peer(k):
        return jnp.bitwise_xor(me, jnp.where(col == 0, k, n - k))

    barrier = pltpu.get_barrier_semaphore()
    for k in range(1, n):
        pl.semaphore_signal(barrier, inc=1, device_id=(jnp.bitwise_xor(me, k), col, slab),
                            device_id_type=mesh_id)
    for k in range(1, parts):
        other = jnp.bitwise_xor(cs, k)
        pl.semaphore_signal(barrier, inc=1, device_id=(me, other // 2, other % 2),
                            device_id_type=mesh_id)
    pl.semaphore_wait(barrier, n - 1 + parts - 1)

    sends = []
    for k in range(1, n):
        t = peer(k)
        c = pltpu.make_async_remote_copy(
            src_ref=p_ref.at[t], dst_ref=rs_buf.at[me], send_sem=rs_send.at[t],
            recv_sem=rs_recv.at[me], device_id=(t, col, slab), device_id_type=mesh_id)
        c.start()
        sends.append(c)
    rs_buf[pl.ds(me, 1)] = p_ref[pl.ds(me, 1)]
    for k in range(1, n):
        s = jnp.bitwise_xor(me, k)
        pltpu.make_async_remote_copy(
            src_ref=p_ref.at[s], dst_ref=rs_buf.at[s], send_sem=rs_send.at[s],
            recv_sem=rs_recv.at[s], device_id=(s, col, slab), device_id_type=mesh_id).wait_recv()
    total = rs_buf[0]
    for s in range(1, n):
        total = total + rs_buf[s]
    ar_buf[pl.ds(cs, 1)] = total[None]
    for k in range(1, parts):
        other = jnp.bitwise_xor(cs, k)
        c = pltpu.make_async_remote_copy(
            src_ref=ar_buf.at[cs], dst_ref=ar_buf.at[cs], send_sem=ar_send.at[other],
            recv_sem=ar_recv.at[cs], device_id=(me, other // 2, other % 2), device_id_type=mesh_id)
        c.start()
        sends.append(c)
    for k in range(1, parts):
        other = jnp.bitwise_xor(cs, k)
        pltpu.make_async_remote_copy(
            src_ref=ar_buf.at[other], dst_ref=ar_buf.at[other], send_sem=ar_send.at[other],
            recv_sem=ar_recv.at[other], device_id=(me, other // 2, other % 2),
            device_id_type=mesh_id).wait_recv()
    total = ar_buf[0]
    for j in range(1, parts):
        total = total + ar_buf[j]
    acc_ref[...] = total
    local = pltpu.make_async_copy(acc_ref, out_ref.at[me], local_sem.at[0])
    local.start()
    for k in range(1, n):
        t = peer(k)
        c = pltpu.make_async_remote_copy(
            src_ref=acc_ref, dst_ref=out_ref.at[me], send_sem=ag_send.at[t],
            recv_sem=ag_recv.at[me], device_id=(t, col, slab), device_id_type=mesh_id)
        c.start()
        sends.append(c)
    for k in range(1, n):
        s = jnp.bitwise_xor(me, k)
        pltpu.make_async_remote_copy(
            src_ref=acc_ref, dst_ref=out_ref.at[s], send_sem=ag_send.at[s],
            recv_sem=ag_recv.at[s], device_id=(s, col, slab), device_id_type=mesh_id).wait_recv()
    for c in sends:
        c.wait_send()
    local.wait()


def lower_psum(partial, n, parts, block=128):
    size = partial.shape[0]
    nb = size // block
    pairs = [(i, j) for i in range(nb) for j in range(i + 1)]
    packed = jnp.concatenate(
        [partial[i * block:(i + 1) * block, j * block:(j + 1) * block] for i, j in pairs], axis=0)
    rows = packed.shape[0] // n
    packed = packed.reshape(n, rows, block)
    reduced = pl.pallas_call(
        functools.partial(reduce_kernel, n, parts),
        out_shape=jax.ShapeDtypeStruct((n, rows, block), jnp.float32),
        in_specs=[pl.BlockSpec(memory_space=pltpu.VMEM)],
        out_specs=pl.BlockSpec(memory_space=pl.ANY),
        scratch_shapes=[
            pltpu.VMEM((n, rows, block), jnp.float32),
            pltpu.VMEM((parts, rows, block), jnp.float32),
            pltpu.VMEM((rows, block), jnp.float32),
            pltpu.SemaphoreType.DMA((n,)),
            pltpu.SemaphoreType.DMA((n,)),
            pltpu.SemaphoreType.DMA((parts,)),
            pltpu.SemaphoreType.DMA((parts,)),
            pltpu.SemaphoreType.DMA((n,)),
            pltpu.SemaphoreType.DMA((n,)),
            pltpu.SemaphoreType.DMA((1,)),
        ],
        compiler_params=pltpu.CompilerParams(collective_id=1, has_side_effects=True),
    )(packed)
    blocks = reduced.reshape(len(pairs), block, block)
    where = {p: k for k, p in enumerate(pairs)}
    zero = jnp.zeros((block, block), jnp.float32)
    lower = jnp.concatenate([
        jnp.concatenate([blocks[where[(i, j)]] if j <= i else zero for j in range(nb)], axis=1)
        for i in range(nb)], axis=0)
    diag = jnp.stack([blocks[where[(i, i)]] for i in range(nb)])
    return lower, diag


def cholesky_solve(a, rhs, block=128):
    n = a.shape[0]
    nb = n // block
    hi = lax.Precision.HIGHEST
    eye = jnp.eye(block, dtype=jnp.float32)
    inverses, panels, factors = [], [], []
    for k in range(nb):
        lo = k * block
        lkk = lax.linalg.cholesky(a[lo:lo + block, lo:lo + block], symmetrize_input=False)
        inv = lax.linalg.triangular_solve(lkk, eye, left_side=True, lower=True)
        factors.append(lkk)
        inverses.append(inv)
        if k < nb - 1:
            panel = jnp.dot(a[lo + block:, lo:lo + block], inv.T, precision=hi)
            panels.append(panel)
            a = a.at[lo + block:, lo + block:].add(-jnp.dot(panel, panel.T, precision=hi))
    ys = []
    tail = rhs
    for k in range(nb):
        y = jnp.dot(inverses[k], tail[:block], precision=hi)
        ys.append(y)
        if k < nb - 1:
            tail = tail[block:] - jnp.dot(panels[k], y, precision=hi)
    solved = jnp.dot(ys[nb - 1], inverses[nb - 1], precision=hi)
    for k in reversed(range(nb - 1)):
        r = ys[k] - jnp.dot(solved, panels[k], precision=hi)
        solved = jnp.concatenate([jnp.dot(r, inverses[k], precision=hi), solved])
    return solved


def shards(n, jacobian, local_energy):
    gathered, energies = exchange(jacobian, local_energy, n)
    energies = energies.reshape(-1)
    samples = energies.shape[0]
    root_count = jnp.sqrt(jnp.float32(samples))
    eps = (energies - jnp.mean(energies)) / root_count
    columns = gathered.reshape(samples, gathered.shape[2], gathered.shape[3])
    slab_count = columns.shape[1]
    width = columns.shape[2]
    values = columns.astype(jnp.float32)
    mean_row = jnp.mean(values, axis=0, keepdims=True)
    centered = (
        ((values - mean_row) / root_count).astype(jnp.bfloat16).reshape(samples, slab_count * width)
    )
    partial_gram = jnp.dot(centered, centered.T, preferred_element_type=jnp.float32)
    parts = lax.psum(1, ("col", "slab"))
    gram, diag = lower_psum(partial_gram, n, parts)
    shift = 0.01 * jnp.trace(gram) / samples
    coeffs = cholesky_solve(gram + shift * jnp.eye(samples, dtype=jnp.float32), eps)
    delta = jnp.sum(coeffs[:, None] * centered.astype(jnp.float32), axis=0)
    hi = lax.Precision.HIGHEST
    blocked = coeffs.reshape(diag.shape[0], diag.shape[1])
    full_c = (jnp.dot(gram, coeffs, precision=hi) + jnp.dot(coeffs, gram, precision=hi)
              - jnp.einsum("bij,bj->bi", diag, blocked, precision=hi).reshape(-1))
    squared = jnp.dot(coeffs, full_c, precision=hi)
    limit = 0.3 * jnp.sqrt(jnp.float32(SLABS * SLAB_COLS))
    scaled = -jnp.minimum(1.0, limit / jnp.sqrt(squared)) * delta
    return scaled.reshape(slab_count, width)


def solution(mesh):
    in_specs = (P("smp", "slab", "col"), P("smp"))
    out_specs = P("slab", ("col", "smp"))
    return jax.shard_map(functools.partial(shards, mesh.shape["smp"]), mesh=mesh,
                         in_specs=in_specs, out_specs=out_specs, check_vma=False)
```

```python
import functools

import jax
import jax.numpy as jnp
from jax import lax
from jax.experimental import pallas as pl
from jax.experimental.pallas import tpu as pltpu
from jax.sharding import PartitionSpec as P

SLABS = 32
SLAB_COLS = 16384


def exchange_kernel(n, width, jac_ref, en_ref, cols_ref, en_all_ref,
                    send_sems, recv_sems, en_send, en_recv, local_sems):
    me = lax.axis_index("smp")
    col = lax.axis_index("col")
    slab = lax.axis_index("slab")

    def piece(t):
        return jac_ref.at[:, :, pl.ds(pl.multiple_of(t * width, width), width)]

    barrier = pltpu.get_barrier_semaphore()
    for k in range(1, n):
        pl.semaphore_signal(barrier, inc=1, device_id=(jnp.bitwise_xor(me, k), col, slab),
                            device_id_type=pl.DeviceIdType.MESH)
    pl.semaphore_wait(barrier, n - 1)
    local = pltpu.make_async_copy(piece(me), cols_ref.at[me], local_sems.at[0])
    local.start()
    local_en = pltpu.make_async_copy(en_ref, en_all_ref.at[me], local_sems.at[1])
    local_en.start()
    sends = []
    order = [i ^ (i // 2) for i in range(1, n)]
    for i in range(n - 1):
        t = jnp.bitwise_xor(me, jnp.where(col == 0, order[i], order[n - 2 - i]))
        dev = (t, col, slab)
        c = pltpu.make_async_remote_copy(
            src_ref=piece(t), dst_ref=cols_ref.at[me],
            send_sem=send_sems.at[t], recv_sem=recv_sems.at[me],
            device_id=dev, device_id_type=pl.DeviceIdType.MESH)
        c.start()
        e = pltpu.make_async_remote_copy(
            src_ref=en_ref, dst_ref=en_all_ref.at[me],
            send_sem=en_send.at[t], recv_sem=en_recv.at[me],
            device_id=dev, device_id_type=pl.DeviceIdType.MESH)
        e.start()
        sends.append((c, e))
    for k in range(1, n):
        s = jnp.bitwise_xor(me, k)
        dev = (s, col, slab)
        pltpu.make_async_remote_copy(
            src_ref=piece(me), dst_ref=cols_ref.at[s],
            send_sem=send_sems.at[s], recv_sem=recv_sems.at[s],
            device_id=dev, device_id_type=pl.DeviceIdType.MESH).wait_recv()
        pltpu.make_async_remote_copy(
            src_ref=en_ref, dst_ref=en_all_ref.at[s],
            send_sem=en_send.at[s], recv_sem=en_recv.at[s],
            device_id=dev, device_id_type=pl.DeviceIdType.MESH).wait_recv()
    for c, e in sends:
        c.wait_send()
        e.wait_send()
    local.wait()
    local_en.wait()


def exchange(jacobian, local_energy, n):
    rows, slabs, cols = jacobian.shape
    width = cols // n
    en = local_energy.reshape(1, rows)
    return pl.pallas_call(
        functools.partial(exchange_kernel, n, width),
        out_shape=(
            jax.ShapeDtypeStruct((n, rows, slabs, width), jacobian.dtype),
            jax.ShapeDtypeStruct((n, 1, rows), local_energy.dtype),
        ),
        in_specs=[pl.BlockSpec(memory_space=pl.ANY)] * 2,
        out_specs=(pl.BlockSpec(memory_space=pl.ANY), pl.BlockSpec(memory_space=pl.ANY)),
        scratch_shapes=[
            pltpu.SemaphoreType.DMA((n,)),
            pltpu.SemaphoreType.DMA((n,)),
            pltpu.SemaphoreType.DMA((n,)),
            pltpu.SemaphoreType.DMA((n,)),
            pltpu.SemaphoreType.DMA((2,)),
        ],
        compiler_params=pltpu.CompilerParams(collective_id=0, has_side_effects=True),
    )(jacobian, en)


def reduce_kernel(n, parts, p_ref, out_ref, rs_buf, ar_buf, acc_ref, rs_send, rs_recv,
                  ar_send, ar_recv, ag_send, ag_recv, local_sem):
    me = lax.axis_index("smp")
    col = lax.axis_index("col")
    slab = lax.axis_index("slab")
    cs = col * 2 + slab
    mesh_id = pl.DeviceIdType.MESH

    def peer(k):
        return jnp.bitwise_xor(me, jnp.where(col == 0, k, n - k))

    barrier = pltpu.get_barrier_semaphore()
    for k in range(1, n):
        pl.semaphore_signal(barrier, inc=1, device_id=(jnp.bitwise_xor(me, k), col, slab),
                            device_id_type=mesh_id)
    for k in range(1, parts):
        other = jnp.bitwise_xor(cs, k)
        pl.semaphore_signal(barrier, inc=1, device_id=(me, other // 2, other % 2),
                            device_id_type=mesh_id)
    pl.semaphore_wait(barrier, n - 1 + parts - 1)

    sends = []
    for k in range(1, n):
        t = peer(k)
        c = pltpu.make_async_remote_copy(
            src_ref=p_ref.at[t], dst_ref=rs_buf.at[me], send_sem=rs_send.at[t],
            recv_sem=rs_recv.at[me], device_id=(t, col, slab), device_id_type=mesh_id)
        c.start()
        sends.append(c)
    rs_buf[pl.ds(me, 1)] = p_ref[pl.ds(me, 1)]
    for k in range(1, n):
        s = jnp.bitwise_xor(me, k)
        pltpu.make_async_remote_copy(
            src_ref=p_ref.at[s], dst_ref=rs_buf.at[s], send_sem=rs_send.at[s],
            recv_sem=rs_recv.at[s], device_id=(s, col, slab), device_id_type=mesh_id).wait_recv()
    total = rs_buf[0]
    for s in range(1, n):
        total = total + rs_buf[s]
    ar_buf[pl.ds(cs, 1)] = total[None]
    for k in range(1, parts):
        other = jnp.bitwise_xor(cs, k)
        c = pltpu.make_async_remote_copy(
            src_ref=ar_buf.at[cs], dst_ref=ar_buf.at[cs], send_sem=ar_send.at[other],
            recv_sem=ar_recv.at[cs], device_id=(me, other // 2, other % 2), device_id_type=mesh_id)
        c.start()
        sends.append(c)
    for k in range(1, parts):
        other = jnp.bitwise_xor(cs, k)
        pltpu.make_async_remote_copy(
            src_ref=ar_buf.at[other], dst_ref=ar_buf.at[other], send_sem=ar_send.at[other],
            recv_sem=ar_recv.at[other], device_id=(me, other // 2, other % 2),
            device_id_type=mesh_id).wait_recv()
    total = ar_buf[0]
    for j in range(1, parts):
        total = total + ar_buf[j]
    acc_ref[...] = total
    local = pltpu.make_async_copy(acc_ref, out_ref.at[me], local_sem.at[0])
    local.start()
    for k in range(1, n):
        t = peer(k)
        c = pltpu.make_async_remote_copy(
            src_ref=acc_ref, dst_ref=out_ref.at[me], send_sem=ag_send.at[t],
            recv_sem=ag_recv.at[me], device_id=(t, col, slab), device_id_type=mesh_id)
        c.start()
        sends.append(c)
    for k in range(1, n):
        s = jnp.bitwise_xor(me, k)
        pltpu.make_async_remote_copy(
            src_ref=acc_ref, dst_ref=out_ref.at[s], send_sem=ag_send.at[s],
            recv_sem=ag_recv.at[s], device_id=(s, col, slab), device_id_type=mesh_id).wait_recv()
    for c in sends:
        c.wait_send()
    local.wait()


def lower_psum(partial, n, parts, block=128):
    size = partial.shape[0]
    nb = size // block
    pairs = [(i, j) for i in range(nb) for j in range(i + 1)]
    packed = jnp.concatenate(
        [partial[i * block:(i + 1) * block, j * block:(j + 1) * block] for i, j in pairs], axis=0)
    rows = packed.shape[0] // n
    packed = packed.reshape(n, rows, block)
    reduced = pl.pallas_call(
        functools.partial(reduce_kernel, n, parts),
        out_shape=jax.ShapeDtypeStruct((n, rows, block), jnp.float32),
        in_specs=[pl.BlockSpec(memory_space=pltpu.VMEM)],
        out_specs=pl.BlockSpec(memory_space=pl.ANY),
        scratch_shapes=[
            pltpu.VMEM((n, rows, block), jnp.float32),
            pltpu.VMEM((parts, rows, block), jnp.float32),
            pltpu.VMEM((rows, block), jnp.float32),
            pltpu.SemaphoreType.DMA((n,)),
            pltpu.SemaphoreType.DMA((n,)),
            pltpu.SemaphoreType.DMA((parts,)),
            pltpu.SemaphoreType.DMA((parts,)),
            pltpu.SemaphoreType.DMA((n,)),
            pltpu.SemaphoreType.DMA((n,)),
            pltpu.SemaphoreType.DMA((1,)),
        ],
        compiler_params=pltpu.CompilerParams(collective_id=1, has_side_effects=True),
    )(packed)
    blocks = reduced.reshape(len(pairs), block, block)
    where = {p: k for k, p in enumerate(pairs)}
    zero = jnp.zeros((block, block), jnp.float32)
    lower = jnp.concatenate([
        jnp.concatenate([blocks[where[(i, j)]] if j <= i else zero for j in range(nb)], axis=1)
        for i in range(nb)], axis=0)
    diag = jnp.stack([blocks[where[(i, i)]] for i in range(nb)])
    return lower, diag


def cholesky_solve(a, rhs, block=128):
    n = a.shape[0]
    nb = n // block
    hi = lax.Precision.HIGHEST
    eye = jnp.eye(block, dtype=jnp.float32)
    inverses, panels, factors = [], [], []
    for k in range(nb):
        lo = k * block
        lkk = lax.linalg.cholesky(a[lo:lo + block, lo:lo + block], symmetrize_input=False)
        inv = lax.linalg.triangular_solve(lkk, eye, left_side=True, lower=True)
        factors.append(lkk)
        inverses.append(inv)
        if k < nb - 1:
            panel = jnp.dot(a[lo + block:, lo:lo + block], inv.T, precision=hi)
            panels.append(panel)
            a = a.at[lo + block:, lo + block:].add(-jnp.dot(panel, panel.T, precision=hi))
    ys = []
    tail = rhs
    for k in range(nb):
        y = jnp.dot(inverses[k], tail[:block], precision=hi)
        ys.append(y)
        if k < nb - 1:
            tail = tail[block:] - jnp.dot(panels[k], y, precision=hi)
    solved = jnp.dot(ys[nb - 1], inverses[nb - 1], precision=hi)
    for k in reversed(range(nb - 1)):
        r = ys[k] - jnp.dot(solved, panels[k], precision=hi)
        solved = jnp.concatenate([jnp.dot(r, inverses[k], precision=hi), solved])
    return solved


def shards(n, jacobian, local_energy):
    gathered, energies = exchange(jacobian, local_energy, n)
    energies = energies.reshape(-1)
    samples = energies.shape[0]
    root_count = jnp.sqrt(jnp.float32(samples))
    eps = (energies - jnp.mean(energies)) / root_count
    columns = gathered.reshape(samples, gathered.shape[2], gathered.shape[3])
    slab_count = columns.shape[1]
    width = columns.shape[2]
    values = columns.astype(jnp.float32)
    mean_row = jnp.mean(values, axis=0, keepdims=True)
    centered = (
        ((values - mean_row) / root_count).astype(jnp.bfloat16).reshape(samples, slab_count * width)
    )
    partial_gram = jnp.dot(centered, centered.T, preferred_element_type=jnp.float32)
    parts = lax.psum(1, ("col", "slab"))
    gram, diag = lower_psum(partial_gram, n, parts)
    shift = 0.01 * jnp.trace(gram) / samples
    coeffs = cholesky_solve(gram + shift * jnp.eye(samples, dtype=jnp.float32), eps)
    delta = jnp.sum(coeffs[:, None] * centered.astype(jnp.float32), axis=0)
    hi = lax.Precision.HIGHEST
    blocked = coeffs.reshape(diag.shape[0], diag.shape[1])
    full_c = (jnp.dot(gram, coeffs, precision=hi) + jnp.dot(coeffs, gram, precision=hi)
              - jnp.einsum("bij,bj->bi", diag, blocked, precision=hi).reshape(-1))
    squared = jnp.dot(coeffs, full_c, precision=hi)
    limit = 0.3 * jnp.sqrt(jnp.float32(SLABS * SLAB_COLS))
    scaled = -jnp.minimum(1.0, limit / jnp.sqrt(squared)) * delta
    return scaled.reshape(slab_count, width)


def solution(mesh):
    in_specs = (P("smp", "slab", "col"), P("smp"))
    out_specs = P("slab", ("col", "smp"))
    return jax.shard_map(functools.partial(shards, mesh.shape["smp"]), mesh=mesh,
                         in_specs=in_specs, out_specs=out_specs, check_vma=False)
```

```python
import functools

import jax
import jax.numpy as jnp
from jax import lax
from jax.experimental import pallas as pl
from jax.experimental.pallas import tpu as pltpu
from jax.sharding import PartitionSpec as P

SLABS = 32
SLAB_COLS = 16384


def exchange_kernel(n, width, jac_ref, en_ref, cols_ref, en_all_ref,
                    send_sems, recv_sems, en_send, en_recv, local_sems):
    me = lax.axis_index("smp")
    col = lax.axis_index("col")
    slab = lax.axis_index("slab")

    def piece(t):
        return jac_ref.at[:, :, pl.ds(pl.multiple_of(t * width, width), width)]

    barrier = pltpu.get_barrier_semaphore()
    for k in range(1, n):
        pl.semaphore_signal(barrier, inc=1, device_id=(jnp.bitwise_xor(me, k), col, slab),
                            device_id_type=pl.DeviceIdType.MESH)
    pl.semaphore_wait(barrier, n - 1)
    local = pltpu.make_async_copy(piece(me), cols_ref.at[me], local_sems.at[0])
    local.start()
    local_en = pltpu.make_async_copy(en_ref, en_all_ref.at[me], local_sems.at[1])
    local_en.start()
    sends = []
    order = [i ^ (i // 2) for i in range(1, n)]
    for i in range(n - 1):
        t = jnp.bitwise_xor(me, jnp.where(col == 0, order[i], order[n - 2 - i]))
        dev = (t, col, slab)
        c = pltpu.make_async_remote_copy(
            src_ref=piece(t), dst_ref=cols_ref.at[me],
            send_sem=send_sems.at[t], recv_sem=recv_sems.at[me],
            device_id=dev, device_id_type=pl.DeviceIdType.MESH)
        c.start()
        e = pltpu.make_async_remote_copy(
            src_ref=en_ref, dst_ref=en_all_ref.at[me],
            send_sem=en_send.at[t], recv_sem=en_recv.at[me],
            device_id=dev, device_id_type=pl.DeviceIdType.MESH)
        e.start()
        sends.append((c, e))
    for k in range(1, n):
        s = jnp.bitwise_xor(me, k)
        dev = (s, col, slab)
        pltpu.make_async_remote_copy(
            src_ref=piece(me), dst_ref=cols_ref.at[s],
            send_sem=send_sems.at[s], recv_sem=recv_sems.at[s],
            device_id=dev, device_id_type=pl.DeviceIdType.MESH).wait_recv()
        pltpu.make_async_remote_copy(
            src_ref=en_ref, dst_ref=en_all_ref.at[s],
            send_sem=en_send.at[s], recv_sem=en_recv.at[s],
            device_id=dev, device_id_type=pl.DeviceIdType.MESH).wait_recv()
    for c, e in sends:
        c.wait_send()
        e.wait_send()
    local.wait()
    local_en.wait()


def exchange(jacobian, local_energy, n):
    rows, slabs, cols = jacobian.shape
    width = cols // n
    en = local_energy.reshape(1, rows)
    return pl.pallas_call(
        functools.partial(exchange_kernel, n, width),
        out_shape=(
            jax.ShapeDtypeStruct((n, rows, slabs, width), jacobian.dtype),
            jax.ShapeDtypeStruct((n, 1, rows), local_energy.dtype),
        ),
        in_specs=[pl.BlockSpec(memory_space=pl.ANY)] * 2,
        out_specs=(pl.BlockSpec(memory_space=pl.ANY), pl.BlockSpec(memory_space=pl.ANY)),
        scratch_shapes=[
            pltpu.SemaphoreType.DMA((n,)),
            pltpu.SemaphoreType.DMA((n,)),
            pltpu.SemaphoreType.DMA((n,)),
            pltpu.SemaphoreType.DMA((n,)),
            pltpu.SemaphoreType.DMA((2,)),
        ],
        compiler_params=pltpu.CompilerParams(collective_id=0, has_side_effects=True),
    )(jacobian, en)


def reduce_kernel(n, parts, p_ref, out_ref, rs_buf, ar_buf, acc_ref, rs_send, rs_recv,
                  ar_send, ar_recv, ag_send, ag_recv, local_sem):
    me = lax.axis_index("smp")
    col = lax.axis_index("col")
    slab = lax.axis_index("slab")
    cs = col * 2 + slab
    mesh_id = pl.DeviceIdType.MESH

    order = [i ^ (i // 2) for i in range(1, n)]

    def peer(k):
        return jnp.bitwise_xor(me, jnp.where(col == 0, order[k - 1], order[n - 1 - k]))

    barrier = pltpu.get_barrier_semaphore()
    for k in range(1, n):
        pl.semaphore_signal(barrier, inc=1, device_id=(jnp.bitwise_xor(me, k), col, slab),
                            device_id_type=mesh_id)
    for k in range(1, parts):
        other = jnp.bitwise_xor(cs, k)
        pl.semaphore_signal(barrier, inc=1, device_id=(me, other // 2, other % 2),
                            device_id_type=mesh_id)
    pl.semaphore_wait(barrier, n - 1 + parts - 1)

    sends = []
    for k in range(1, n):
        t = peer(k)
        c = pltpu.make_async_remote_copy(
            src_ref=p_ref.at[t], dst_ref=rs_buf.at[me], send_sem=rs_send.at[t],
            recv_sem=rs_recv.at[me], device_id=(t, col, slab), device_id_type=mesh_id)
        c.start()
        sends.append(c)
    rs_buf[pl.ds(me, 1)] = p_ref[pl.ds(me, 1)]
    for k in range(1, n):
        s = jnp.bitwise_xor(me, k)
        pltpu.make_async_remote_copy(
            src_ref=p_ref.at[s], dst_ref=rs_buf.at[s], send_sem=rs_send.at[s],
            recv_sem=rs_recv.at[s], device_id=(s, col, slab), device_id_type=mesh_id).wait_recv()
    total = rs_buf[0]
    for s in range(1, n):
        total = total + rs_buf[s]
    ar_buf[pl.ds(cs, 1)] = total[None]
    for k in range(1, parts):
        other = jnp.bitwise_xor(cs, k)
        c = pltpu.make_async_remote_copy(
            src_ref=ar_buf.at[cs], dst_ref=ar_buf.at[cs], send_sem=ar_send.at[other],
            recv_sem=ar_recv.at[cs], device_id=(me, other // 2, other % 2), device_id_type=mesh_id)
        c.start()
        sends.append(c)
    for k in range(1, parts):
        other = jnp.bitwise_xor(cs, k)
        pltpu.make_async_remote_copy(
            src_ref=ar_buf.at[other], dst_ref=ar_buf.at[other], send_sem=ar_send.at[other],
            recv_sem=ar_recv.at[other], device_id=(me, other // 2, other % 2),
            device_id_type=mesh_id).wait_recv()
    total = ar_buf[0]
    for j in range(1, parts):
        total = total + ar_buf[j]
    acc_ref[...] = total
    local = pltpu.make_async_copy(acc_ref, out_ref.at[me], local_sem.at[0])
    local.start()
    for k in range(1, n):
        t = peer(k)
        c = pltpu.make_async_remote_copy(
            src_ref=acc_ref, dst_ref=out_ref.at[me], send_sem=ag_send.at[t],
            recv_sem=ag_recv.at[me], device_id=(t, col, slab), device_id_type=mesh_id)
        c.start()
        sends.append(c)
    for k in range(1, n):
        s = jnp.bitwise_xor(me, k)
        pltpu.make_async_remote_copy(
            src_ref=acc_ref, dst_ref=out_ref.at[s], send_sem=ag_send.at[s],
            recv_sem=ag_recv.at[s], device_id=(s, col, slab), device_id_type=mesh_id).wait_recv()
    for c in sends:
        c.wait_send()
    local.wait()


def lower_psum(partial, n, parts, block=128):
    size = partial.shape[0]
    nb = size // block
    pairs = [(i, j) for i in range(nb) for j in range(i + 1)]
    packed = jnp.concatenate(
        [partial[i * block:(i + 1) * block, j * block:(j + 1) * block] for i, j in pairs], axis=0)
    rows = packed.shape[0] // n
    packed = packed.reshape(n, rows, block)
    reduced = pl.pallas_call(
        functools.partial(reduce_kernel, n, parts),
        out_shape=jax.ShapeDtypeStruct((n, rows, block), jnp.float32),
        in_specs=[pl.BlockSpec(memory_space=pltpu.VMEM)],
        out_specs=pl.BlockSpec(memory_space=pl.ANY),
        scratch_shapes=[
            pltpu.VMEM((n, rows, block), jnp.float32),
            pltpu.VMEM((parts, rows, block), jnp.float32),
            pltpu.VMEM((rows, block), jnp.float32),
            pltpu.SemaphoreType.DMA((n,)),
            pltpu.SemaphoreType.DMA((n,)),
            pltpu.SemaphoreType.DMA((parts,)),
            pltpu.SemaphoreType.DMA((parts,)),
            pltpu.SemaphoreType.DMA((n,)),
            pltpu.SemaphoreType.DMA((n,)),
            pltpu.SemaphoreType.DMA((1,)),
        ],
        compiler_params=pltpu.CompilerParams(collective_id=1, has_side_effects=True),
    )(packed)
    blocks = reduced.reshape(len(pairs), block, block)
    where = {p: k for k, p in enumerate(pairs)}
    zero = jnp.zeros((block, block), jnp.float32)
    lower = jnp.concatenate([
        jnp.concatenate([blocks[where[(i, j)]] if j <= i else zero for j in range(nb)], axis=1)
        for i in range(nb)], axis=0)
    diag = jnp.stack([blocks[where[(i, i)]] for i in range(nb)])
    return lower, diag


def cholesky_solve(a, rhs, block=128):
    n = a.shape[0]
    nb = n // block
    hi = lax.Precision.HIGHEST
    eye = jnp.eye(block, dtype=jnp.float32)
    inverses, panels, factors = [], [], []
    for k in range(nb):
        lo = k * block
        lkk = lax.linalg.cholesky(a[lo:lo + block, lo:lo + block], symmetrize_input=False)
        inv = lax.linalg.triangular_solve(lkk, eye, left_side=True, lower=True)
        factors.append(lkk)
        inverses.append(inv)
        if k < nb - 1:
            panel = jnp.dot(a[lo + block:, lo:lo + block], inv.T, precision=hi)
            panels.append(panel)
            a = a.at[lo + block:, lo + block:].add(-jnp.dot(panel, panel.T, precision=hi))
    ys = []
    tail = rhs
    for k in range(nb):
        y = jnp.dot(inverses[k], tail[:block], precision=hi)
        ys.append(y)
        if k < nb - 1:
            tail = tail[block:] - jnp.dot(panels[k], y, precision=hi)
    solved = jnp.dot(ys[nb - 1], inverses[nb - 1], precision=hi)
    for k in reversed(range(nb - 1)):
        r = ys[k] - jnp.dot(solved, panels[k], precision=hi)
        solved = jnp.concatenate([jnp.dot(r, inverses[k], precision=hi), solved])
    return solved


def shards(n, jacobian, local_energy):
    gathered, energies = exchange(jacobian, local_energy, n)
    energies = energies.reshape(-1)
    samples = energies.shape[0]
    root_count = jnp.sqrt(jnp.float32(samples))
    eps = (energies - jnp.mean(energies)) / root_count
    columns = gathered.reshape(samples, gathered.shape[2], gathered.shape[3])
    slab_count = columns.shape[1]
    width = columns.shape[2]
    values = columns.astype(jnp.float32)
    mean_row = jnp.mean(values, axis=0, keepdims=True)
    centered = (
        ((values - mean_row) / root_count).astype(jnp.bfloat16).reshape(samples, slab_count * width)
    )
    partial_gram = jnp.dot(centered, centered.T, preferred_element_type=jnp.float32)
    parts = lax.psum(1, ("col", "slab"))
    gram, diag = lower_psum(partial_gram, n, parts)
    shift = 0.01 * jnp.trace(gram) / samples
    coeffs = cholesky_solve(gram + shift * jnp.eye(samples, dtype=jnp.float32), eps)
    delta = jnp.sum(coeffs[:, None] * centered.astype(jnp.float32), axis=0)
    hi = lax.Precision.HIGHEST
    blocked = coeffs.reshape(diag.shape[0], diag.shape[1])
    full_c = (jnp.dot(gram, coeffs, precision=hi) + jnp.dot(coeffs, gram, precision=hi)
              - jnp.einsum("bij,bj->bi", diag, blocked, precision=hi).reshape(-1))
    squared = jnp.dot(coeffs, full_c, precision=hi)
    limit = 0.3 * jnp.sqrt(jnp.float32(SLABS * SLAB_COLS))
    scaled = -jnp.minimum(1.0, limit / jnp.sqrt(squared)) * delta
    return scaled.reshape(slab_count, width)


def solution(mesh):
    in_specs = (P("smp", "slab", "col"), P("smp"))
    out_specs = P("slab", ("col", "smp"))
    return jax.shard_map(functools.partial(shards, mesh.shape["smp"]), mesh=mesh,
                         in_specs=in_specs, out_specs=out_specs, check_vma=False)
```

```python
import functools

import jax
import jax.numpy as jnp
from jax import lax
from jax.experimental import pallas as pl
from jax.experimental.pallas import tpu as pltpu
from jax.sharding import PartitionSpec as P

SLABS = 32
SLAB_COLS = 16384


def exchange_kernel(n, width, jac_ref, en_ref, cols_ref, en_all_ref,
                    send_sems, recv_sems, en_send, en_recv, local_sems):
    me = lax.axis_index("smp")
    col = lax.axis_index("col")
    slab = lax.axis_index("slab")

    def piece(t):
        return jac_ref.at[:, :, pl.ds(pl.multiple_of(t * width, width), width)]

    barrier = pltpu.get_barrier_semaphore()
    for k in range(1, n):
        pl.semaphore_signal(barrier, inc=1, device_id=(jnp.bitwise_xor(me, k), col, slab),
                            device_id_type=pl.DeviceIdType.MESH)
    pl.semaphore_wait(barrier, n - 1)
    local = pltpu.make_async_copy(piece(me), cols_ref.at[me], local_sems.at[0])
    local.start()
    local_en = pltpu.make_async_copy(en_ref, en_all_ref.at[me], local_sems.at[1])
    local_en.start()
    sends = []
    order = [i ^ (i // 2) for i in range(1, n)]
    for i in range(n - 1):
        t = jnp.bitwise_xor(me, jnp.where(col == 0, order[i], order[n - 2 - i]))
        dev = (t, col, slab)
        c = pltpu.make_async_remote_copy(
            src_ref=piece(t), dst_ref=cols_ref.at[me],
            send_sem=send_sems.at[t], recv_sem=recv_sems.at[me],
            device_id=dev, device_id_type=pl.DeviceIdType.MESH)
        c.start()
        e = pltpu.make_async_remote_copy(
            src_ref=en_ref, dst_ref=en_all_ref.at[me],
            send_sem=en_send.at[t], recv_sem=en_recv.at[me],
            device_id=dev, device_id_type=pl.DeviceIdType.MESH)
        e.start()
        sends.append((c, e))
    for k in range(1, n):
        s = jnp.bitwise_xor(me, k)
        dev = (s, col, slab)
        pltpu.make_async_remote_copy(
            src_ref=piece(me), dst_ref=cols_ref.at[s],
            send_sem=send_sems.at[s], recv_sem=recv_sems.at[s],
            device_id=dev, device_id_type=pl.DeviceIdType.MESH).wait_recv()
        pltpu.make_async_remote_copy(
            src_ref=en_ref, dst_ref=en_all_ref.at[s],
            send_sem=en_send.at[s], recv_sem=en_recv.at[s],
            device_id=dev, device_id_type=pl.DeviceIdType.MESH).wait_recv()
    for c, e in sends:
        c.wait_send()
        e.wait_send()
    local.wait()
    local_en.wait()


def exchange(jacobian, local_energy, n):
    rows, slabs, cols = jacobian.shape
    width = cols // n
    en = local_energy.reshape(1, rows)
    return pl.pallas_call(
        functools.partial(exchange_kernel, n, width),
        out_shape=(
            jax.ShapeDtypeStruct((n, rows, slabs, width), jacobian.dtype),
            jax.ShapeDtypeStruct((n, 1, rows), local_energy.dtype),
        ),
        in_specs=[pl.BlockSpec(memory_space=pl.ANY)] * 2,
        out_specs=(pl.BlockSpec(memory_space=pl.ANY), pl.BlockSpec(memory_space=pl.ANY)),
        scratch_shapes=[
            pltpu.SemaphoreType.DMA((n,)),
            pltpu.SemaphoreType.DMA((n,)),
            pltpu.SemaphoreType.DMA((n,)),
            pltpu.SemaphoreType.DMA((n,)),
            pltpu.SemaphoreType.DMA((2,)),
        ],
        compiler_params=pltpu.CompilerParams(collective_id=0, has_side_effects=True),
    )(jacobian, en)


def reduce_kernel(n, parts, p_ref, out_ref, rs_buf, ar_buf, acc_ref, rs_send, rs_recv,
                  ar_send, ar_recv, ag_send, ag_recv, local_sem):
    me = lax.axis_index("smp")
    col = lax.axis_index("col")
    slab = lax.axis_index("slab")
    cs = col * 2 + slab
    mesh_id = pl.DeviceIdType.MESH

    def peer(k):
        return jnp.bitwise_xor(me, jnp.where(col == 0, k, n - k))

    barrier = pltpu.get_barrier_semaphore()
    for k in range(1, n):
        pl.semaphore_signal(barrier, inc=1, device_id=(jnp.bitwise_xor(me, k), col, slab),
                            device_id_type=mesh_id)
    for k in range(1, parts):
        other = jnp.bitwise_xor(cs, k)
        pl.semaphore_signal(barrier, inc=1, device_id=(me, other // 2, other % 2),
                            device_id_type=mesh_id)
    pl.semaphore_wait(barrier, n - 1 + parts - 1)

    sends = []
    for k in range(1, n):
        t = peer(k)
        c = pltpu.make_async_remote_copy(
            src_ref=p_ref.at[t], dst_ref=rs_buf.at[me], send_sem=rs_send.at[t],
            recv_sem=rs_recv.at[me], device_id=(t, col, slab), device_id_type=mesh_id)
        c.start()
        sends.append(c)
    rs_buf[pl.ds(me, 1)] = p_ref[pl.ds(me, 1)]
    for k in range(1, n):
        s = jnp.bitwise_xor(me, k)
        pltpu.make_async_remote_copy(
            src_ref=p_ref.at[s], dst_ref=rs_buf.at[s], send_sem=rs_send.at[s],
            recv_sem=rs_recv.at[s], device_id=(s, col, slab), device_id_type=mesh_id).wait_recv()
    total = rs_buf[0]
    for s in range(1, n):
        total = total + rs_buf[s]
    ar_buf[pl.ds(cs, 1)] = total[None]
    for k in range(1, parts):
        other = jnp.bitwise_xor(cs, k)
        c = pltpu.make_async_remote_copy(
            src_ref=ar_buf.at[cs], dst_ref=ar_buf.at[cs], send_sem=ar_send.at[other],
            recv_sem=ar_recv.at[cs], device_id=(me, other // 2, other % 2), device_id_type=mesh_id)
        c.start()
        sends.append(c)
    for k in range(1, parts):
        other = jnp.bitwise_xor(cs, k)
        pltpu.make_async_remote_copy(
            src_ref=ar_buf.at[other], dst_ref=ar_buf.at[other], send_sem=ar_send.at[other],
            recv_sem=ar_recv.at[other], device_id=(me, other // 2, other % 2),
            device_id_type=mesh_id).wait_recv()
    total = ar_buf[0]
    for j in range(1, parts):
        total = total + ar_buf[j]
    acc_ref[...] = total
    local = pltpu.make_async_copy(acc_ref, out_ref.at[me], local_sem.at[0])
    local.start()
    for k in range(1, n):
        t = peer(k)
        c = pltpu.make_async_remote_copy(
            src_ref=acc_ref, dst_ref=out_ref.at[me], send_sem=ag_send.at[t],
            recv_sem=ag_recv.at[me], device_id=(t, col, slab), device_id_type=mesh_id)
        c.start()
        sends.append(c)
    for k in range(1, n):
        s = jnp.bitwise_xor(me, k)
        pltpu.make_async_remote_copy(
            src_ref=acc_ref, dst_ref=out_ref.at[s], send_sem=ag_send.at[s],
            recv_sem=ag_recv.at[s], device_id=(s, col, slab), device_id_type=mesh_id).wait_recv()
    for c in sends:
        c.wait_send()
    local.wait()


def lower_psum(partial, n, parts, block=128):
    size = partial.shape[0]
    nb = size // block
    pairs = [(i, j) for i in range(nb) for j in range(i + 1)]
    packed = jnp.concatenate(
        [partial[i * block:(i + 1) * block, j * block:(j + 1) * block] for i, j in pairs], axis=0)
    rows = packed.shape[0] // n
    packed = packed.reshape(n, rows, block)
    reduced = pl.pallas_call(
        functools.partial(reduce_kernel, n, parts),
        out_shape=jax.ShapeDtypeStruct((n, rows, block), jnp.float32),
        in_specs=[pl.BlockSpec(memory_space=pltpu.VMEM)],
        out_specs=pl.BlockSpec(memory_space=pl.ANY),
        scratch_shapes=[
            pltpu.VMEM((n, rows, block), jnp.float32),
            pltpu.VMEM((parts, rows, block), jnp.float32),
            pltpu.VMEM((rows, block), jnp.float32),
            pltpu.SemaphoreType.DMA((n,)),
            pltpu.SemaphoreType.DMA((n,)),
            pltpu.SemaphoreType.DMA((parts,)),
            pltpu.SemaphoreType.DMA((parts,)),
            pltpu.SemaphoreType.DMA((n,)),
            pltpu.SemaphoreType.DMA((n,)),
            pltpu.SemaphoreType.DMA((1,)),
        ],
        compiler_params=pltpu.CompilerParams(collective_id=1, has_side_effects=True),
    )(packed)
    blocks = reduced.reshape(len(pairs), block, block)
    where = {p: k for k, p in enumerate(pairs)}
    zero = jnp.zeros((block, block), jnp.float32)
    lower = jnp.concatenate([
        jnp.concatenate([blocks[where[(i, j)]] if j <= i else zero for j in range(nb)], axis=1)
        for i in range(nb)], axis=0)
    diag = jnp.stack([blocks[where[(i, i)]] for i in range(nb)])
    return lower, diag


def cholesky_solve(a, rhs, shift, block=128):
    n = a.shape[0]
    nb = n // block
    hi = lax.Precision.HIGHEST
    eye = jnp.eye(block, dtype=jnp.float32)
    inverses, panels, factors = [], [], []
    for k in range(nb):
        lo = k * block
        lkk = lax.linalg.cholesky(a[lo:lo + block, lo:lo + block] + shift * eye,
                                  symmetrize_input=False)
        inv = lax.linalg.triangular_solve(lkk, eye, left_side=True, lower=True)
        factors.append(lkk)
        inverses.append(inv)
        if k < nb - 1:
            panel = jnp.dot(a[lo + block:, lo:lo + block], inv.T, precision=hi)
            panels.append(panel)
            a = a.at[lo + block:, lo + block:].add(-jnp.dot(panel, panel.T, precision=hi))
    ys = []
    tail = rhs
    for k in range(nb):
        y = jnp.dot(inverses[k], tail[:block], precision=hi)
        ys.append(y)
        if k < nb - 1:
            tail = tail[block:] - jnp.dot(panels[k], y, precision=hi)
    solved = jnp.dot(ys[nb - 1], inverses[nb - 1], precision=hi)
    for k in reversed(range(nb - 1)):
        r = ys[k] - jnp.dot(solved, panels[k], precision=hi)
        solved = jnp.concatenate([jnp.dot(r, inverses[k], precision=hi), solved])
    return solved


def shards(n, jacobian, local_energy):
    gathered, energies = exchange(jacobian, local_energy, n)
    energies = energies.reshape(-1)
    samples = energies.shape[0]
    root_count = jnp.sqrt(jnp.float32(samples))
    eps = (energies - jnp.mean(energies)) / root_count
    columns = gathered.reshape(samples, gathered.shape[2], gathered.shape[3])
    slab_count = columns.shape[1]
    width = columns.shape[2]
    values = columns.astype(jnp.float32)
    mean_row = jnp.mean(values, axis=0, keepdims=True)
    centered = (
        ((values - mean_row) / root_count).astype(jnp.bfloat16).reshape(samples, slab_count * width)
    )
    partial_gram = jnp.dot(centered, centered.T, preferred_element_type=jnp.float32)
    parts = lax.psum(1, ("col", "slab"))
    gram, diag = lower_psum(partial_gram, n, parts)
    shift = 0.01 * jnp.sum(jnp.trace(diag, axis1=1, axis2=2)) / samples
    coeffs = cholesky_solve(gram, eps, shift)
    delta = jnp.sum(coeffs[:, None] * centered.astype(jnp.float32), axis=0)
    hi = lax.Precision.HIGHEST
    blocked = coeffs.reshape(diag.shape[0], diag.shape[1])
    full_c = (jnp.dot(gram, coeffs, precision=hi) + jnp.dot(coeffs, gram, precision=hi)
              - jnp.einsum("bij,bj->bi", diag, blocked, precision=hi).reshape(-1))
    squared = jnp.dot(coeffs, full_c, precision=hi)
    limit = 0.3 * jnp.sqrt(jnp.float32(SLABS * SLAB_COLS))
    scaled = -jnp.minimum(1.0, limit / jnp.sqrt(squared)) * delta
    return scaled.reshape(slab_count, width)


def solution(mesh):
    in_specs = (P("smp", "slab", "col"), P("smp"))
    out_specs = P("slab", ("col", "smp"))
    return jax.shard_map(functools.partial(shards, mesh.shape["smp"]), mesh=mesh,
                         in_specs=in_specs, out_specs=out_specs, check_vma=False)
```

```python
import functools

import jax
import jax.numpy as jnp
from jax import lax
from jax.experimental import pallas as pl
from jax.experimental.pallas import tpu as pltpu
from jax.sharding import PartitionSpec as P

SLABS = 32
SLAB_COLS = 16384


def exchange_kernel(n, width, jac_ref, en_ref, cols_ref, en_all_ref,
                    send_sems, recv_sems, en_send, en_recv, local_sems):
    me = lax.axis_index("smp")
    col = lax.axis_index("col")
    slab = lax.axis_index("slab")

    def piece(t):
        return jac_ref.at[:, :, pl.ds(pl.multiple_of(t * width, width), width)]

    barrier = pltpu.get_barrier_semaphore()
    for k in range(1, n):
        pl.semaphore_signal(barrier, inc=1, device_id=(jnp.bitwise_xor(me, k), col, slab),
                            device_id_type=pl.DeviceIdType.MESH)
    pl.semaphore_wait(barrier, n - 1)
    local = pltpu.make_async_copy(piece(me), cols_ref.at[me], local_sems.at[0])
    local.start()
    local_en = pltpu.make_async_copy(en_ref, en_all_ref.at[me], local_sems.at[1])
    local_en.start()
    sends = []
    order = [i ^ (i // 2) for i in range(1, n)]
    for i in range(n - 1):
        t = jnp.bitwise_xor(me, jnp.where(col == 0, order[i], order[n - 2 - i]))
        dev = (t, col, slab)
        c = pltpu.make_async_remote_copy(
            src_ref=piece(t), dst_ref=cols_ref.at[me],
            send_sem=send_sems.at[t], recv_sem=recv_sems.at[me],
            device_id=dev, device_id_type=pl.DeviceIdType.MESH)
        c.start()
        e = pltpu.make_async_remote_copy(
            src_ref=en_ref, dst_ref=en_all_ref.at[me],
            send_sem=en_send.at[t], recv_sem=en_recv.at[me],
            device_id=dev, device_id_type=pl.DeviceIdType.MESH)
        e.start()
        sends.append((c, e))
    for k in range(1, n):
        s = jnp.bitwise_xor(me, k)
        dev = (s, col, slab)
        pltpu.make_async_remote_copy(
            src_ref=piece(me), dst_ref=cols_ref.at[s],
            send_sem=send_sems.at[s], recv_sem=recv_sems.at[s],
            device_id=dev, device_id_type=pl.DeviceIdType.MESH).wait_recv()
        pltpu.make_async_remote_copy(
            src_ref=en_ref, dst_ref=en_all_ref.at[s],
            send_sem=en_send.at[s], recv_sem=en_recv.at[s],
            device_id=dev, device_id_type=pl.DeviceIdType.MESH).wait_recv()
    for c, e in sends:
        c.wait_send()
        e.wait_send()
    local.wait()
    local_en.wait()


def exchange(jacobian, local_energy, n):
    rows, slabs, cols = jacobian.shape
    width = cols // n
    en = local_energy.reshape(1, rows)
    return pl.pallas_call(
        functools.partial(exchange_kernel, n, width),
        out_shape=(
            jax.ShapeDtypeStruct((n, rows, slabs, width), jacobian.dtype),
            jax.ShapeDtypeStruct((n, 1, rows), local_energy.dtype),
        ),
        in_specs=[pl.BlockSpec(memory_space=pl.ANY)] * 2,
        out_specs=(pl.BlockSpec(memory_space=pl.ANY), pl.BlockSpec(memory_space=pl.ANY)),
        scratch_shapes=[
            pltpu.SemaphoreType.DMA((n,)),
            pltpu.SemaphoreType.DMA((n,)),
            pltpu.SemaphoreType.DMA((n,)),
            pltpu.SemaphoreType.DMA((n,)),
            pltpu.SemaphoreType.DMA((2,)),
        ],
        compiler_params=pltpu.CompilerParams(collective_id=0, has_side_effects=True),
    )(jacobian, en)


def reduce_kernel(n, parts, p_ref, out_ref, rs_buf, ar_buf, acc_ref, rs_send, rs_recv,
                  ar_send, ar_recv, ag_send, ag_recv, local_sem):
    me = lax.axis_index("smp")
    col = lax.axis_index("col")
    slab = lax.axis_index("slab")
    cs = col * 2 + slab
    mesh_id = pl.DeviceIdType.MESH

    def peer(k):
        return jnp.bitwise_xor(me, jnp.where(col == 0, k, n - k))

    barrier = pltpu.get_barrier_semaphore()
    for k in range(1, n):
        pl.semaphore_signal(barrier, inc=1, device_id=(jnp.bitwise_xor(me, k), col, slab),
                            device_id_type=mesh_id)
    for k in range(1, parts):
        other = jnp.bitwise_xor(cs, k)
        pl.semaphore_signal(barrier, inc=1, device_id=(me, other // 2, other % 2),
                            device_id_type=mesh_id)
    pl.semaphore_wait(barrier, n - 1 + parts - 1)

    sends = []
    for k in range(1, n):
        t = peer(k)
        c = pltpu.make_async_remote_copy(
            src_ref=p_ref.at[t], dst_ref=rs_buf.at[me], send_sem=rs_send.at[t],
            recv_sem=rs_recv.at[me], device_id=(t, col, slab), device_id_type=mesh_id)
        c.start()
        sends.append(c)
    rs_buf[pl.ds(me, 1)] = p_ref[pl.ds(me, 1)]
    for k in range(1, n):
        s = jnp.bitwise_xor(me, k)
        pltpu.make_async_remote_copy(
            src_ref=p_ref.at[s], dst_ref=rs_buf.at[s], send_sem=rs_send.at[s],
            recv_sem=rs_recv.at[s], device_id=(s, col, slab), device_id_type=mesh_id).wait_recv()
    total = rs_buf[0]
    for s in range(1, n):
        total = total + rs_buf[s]
    ar_buf[pl.ds(cs, 1)] = total[None]
    for k in range(1, parts):
        other = jnp.bitwise_xor(cs, k)
        c = pltpu.make_async_remote_copy(
            src_ref=ar_buf.at[cs], dst_ref=ar_buf.at[cs], send_sem=ar_send.at[other],
            recv_sem=ar_recv.at[cs], device_id=(me, other // 2, other % 2), device_id_type=mesh_id)
        c.start()
        sends.append(c)
    for k in range(1, parts):
        other = jnp.bitwise_xor(cs, k)
        pltpu.make_async_remote_copy(
            src_ref=ar_buf.at[other], dst_ref=ar_buf.at[other], send_sem=ar_send.at[other],
            recv_sem=ar_recv.at[other], device_id=(me, other // 2, other % 2),
            device_id_type=mesh_id).wait_recv()
    total = ar_buf[0]
    for j in range(1, parts):
        total = total + ar_buf[j]
    acc_ref[...] = total
    local = pltpu.make_async_copy(acc_ref, out_ref.at[me], local_sem.at[0])
    local.start()
    for k in range(1, n):
        t = peer(k)
        c = pltpu.make_async_remote_copy(
            src_ref=acc_ref, dst_ref=out_ref.at[me], send_sem=ag_send.at[t],
            recv_sem=ag_recv.at[me], device_id=(t, col, slab), device_id_type=mesh_id)
        c.start()
        sends.append(c)
    for k in range(1, n):
        s = jnp.bitwise_xor(me, k)
        pltpu.make_async_remote_copy(
            src_ref=acc_ref, dst_ref=out_ref.at[s], send_sem=ag_send.at[s],
            recv_sem=ag_recv.at[s], device_id=(s, col, slab), device_id_type=mesh_id).wait_recv()
    for c in sends:
        c.wait_send()
    local.wait()


def lower_psum(partial, n, parts, block=128):
    size = partial[-1].shape[1]
    nb = size // block
    pairs = [(i, j) for i in range(nb) for j in range(i + 1)]
    packed = jnp.concatenate(
        [partial[i][:, j * block:(j + 1) * block] for i, j in pairs], axis=0)
    rows = packed.shape[0] // n
    packed = packed.reshape(n, rows, block)
    reduced = pl.pallas_call(
        functools.partial(reduce_kernel, n, parts),
        out_shape=jax.ShapeDtypeStruct((n, rows, block), jnp.float32),
        in_specs=[pl.BlockSpec(memory_space=pltpu.VMEM)],
        out_specs=pl.BlockSpec(memory_space=pl.ANY),
        scratch_shapes=[
            pltpu.VMEM((n, rows, block), jnp.float32),
            pltpu.VMEM((parts, rows, block), jnp.float32),
            pltpu.VMEM((rows, block), jnp.float32),
            pltpu.SemaphoreType.DMA((n,)),
            pltpu.SemaphoreType.DMA((n,)),
            pltpu.SemaphoreType.DMA((parts,)),
            pltpu.SemaphoreType.DMA((parts,)),
            pltpu.SemaphoreType.DMA((n,)),
            pltpu.SemaphoreType.DMA((n,)),
            pltpu.SemaphoreType.DMA((1,)),
        ],
        compiler_params=pltpu.CompilerParams(collective_id=1, has_side_effects=True),
    )(packed)
    blocks = reduced.reshape(len(pairs), block, block)
    where = {p: k for k, p in enumerate(pairs)}
    zero = jnp.zeros((block, block), jnp.float32)
    lower = jnp.concatenate([
        jnp.concatenate([blocks[where[(i, j)]] if j <= i else zero for j in range(nb)], axis=1)
        for i in range(nb)], axis=0)
    diag = jnp.stack([blocks[where[(i, i)]] for i in range(nb)])
    return lower, diag


def cholesky_solve(a, rhs, block=128):
    n = a.shape[0]
    nb = n // block
    hi = lax.Precision.HIGHEST
    eye = jnp.eye(block, dtype=jnp.float32)
    inverses, panels, factors = [], [], []
    for k in range(nb):
        lo = k * block
        lkk = lax.linalg.cholesky(a[lo:lo + block, lo:lo + block], symmetrize_input=False)
        inv = lax.linalg.triangular_solve(lkk, eye, left_side=True, lower=True)
        factors.append(lkk)
        inverses.append(inv)
        if k < nb - 1:
            panel = jnp.dot(a[lo + block:, lo:lo + block], inv.T, precision=hi)
            panels.append(panel)
            a = a.at[lo + block:, lo + block:].add(-jnp.dot(panel, panel.T, precision=hi))
    ys = []
    tail = rhs
    for k in range(nb):
        y = jnp.dot(inverses[k], tail[:block], precision=hi)
        ys.append(y)
        if k < nb - 1:
            tail = tail[block:] - jnp.dot(panels[k], y, precision=hi)
    solved = jnp.dot(ys[nb - 1], inverses[nb - 1], precision=hi)
    for k in reversed(range(nb - 1)):
        r = ys[k] - jnp.dot(solved, panels[k], precision=hi)
        solved = jnp.concatenate([jnp.dot(r, inverses[k], precision=hi), solved])
    return solved


def shards(n, jacobian, local_energy):
    gathered, energies = exchange(jacobian, local_energy, n)
    energies = energies.reshape(-1)
    samples = energies.shape[0]
    root_count = jnp.sqrt(jnp.float32(samples))
    eps = (energies - jnp.mean(energies)) / root_count
    columns = gathered.reshape(samples, gathered.shape[2], gathered.shape[3])
    slab_count = columns.shape[1]
    width = columns.shape[2]
    values = columns.astype(jnp.float32)
    mean_row = jnp.mean(values, axis=0, keepdims=True)
    centered = (
        ((values - mean_row) / root_count).astype(jnp.bfloat16).reshape(samples, slab_count * width)
    )
    strips = [jnp.dot(centered[i * 128:(i + 1) * 128], centered[:(i + 1) * 128].T,
                      preferred_element_type=jnp.float32) for i in range(samples // 128)]
    parts = lax.psum(1, ("col", "slab"))
    gram, diag = lower_psum(strips, n, parts)
    shift = 0.01 * jnp.trace(gram) / samples
    coeffs = cholesky_solve(gram + shift * jnp.eye(samples, dtype=jnp.float32), eps)
    delta = jnp.sum(coeffs[:, None] * centered.astype(jnp.float32), axis=0)
    hi = lax.Precision.HIGHEST
    blocked = coeffs.reshape(diag.shape[0], diag.shape[1])
    full_c = (jnp.dot(gram, coeffs, precision=hi) + jnp.dot(coeffs, gram, precision=hi)
              - jnp.einsum("bij,bj->bi", diag, blocked, precision=hi).reshape(-1))
    squared = jnp.dot(coeffs, full_c, precision=hi)
    limit = 0.3 * jnp.sqrt(jnp.float32(SLABS * SLAB_COLS))
    scaled = -jnp.minimum(1.0, limit / jnp.sqrt(squared)) * delta
    return scaled.reshape(slab_count, width)


def solution(mesh):
    in_specs = (P("smp", "slab", "col"), P("smp"))
    out_specs = P("slab", ("col", "smp"))
    return jax.shard_map(functools.partial(shards, mesh.shape["smp"]), mesh=mesh,
                         in_specs=in_specs, out_specs=out_specs, check_vma=False)
```

```python
import functools

import jax
import jax.numpy as jnp
from jax import lax
from jax.experimental import pallas as pl
from jax.experimental.pallas import tpu as pltpu
from jax.sharding import PartitionSpec as P

SLABS = 32
SLAB_COLS = 16384


def exchange_kernel(n, width, jac_ref, en_ref, cols_ref, en_all_ref,
                    send_sems, recv_sems, en_send, en_recv, local_sems):
    me = lax.axis_index("smp")
    col = lax.axis_index("col")
    slab = lax.axis_index("slab")

    def piece(t):
        return jac_ref.at[:, :, pl.ds(pl.multiple_of(t * width, width), width)]

    barrier = pltpu.get_barrier_semaphore()
    for k in range(1, n):
        pl.semaphore_signal(barrier, inc=1, device_id=(jnp.bitwise_xor(me, k), col, slab),
                            device_id_type=pl.DeviceIdType.MESH)
    pl.semaphore_wait(barrier, n - 1)
    local = pltpu.make_async_copy(piece(me), cols_ref.at[me], local_sems.at[0])
    local.start()
    local_en = pltpu.make_async_copy(en_ref, en_all_ref.at[me], local_sems.at[1])
    local_en.start()
    sends = []
    order = [i ^ (i // 2) for i in range(1, n)]
    for i in range(n - 1):
        t = jnp.bitwise_xor(me, jnp.where(col == 0, order[i], order[n - 2 - i]))
        dev = (t, col, slab)
        c = pltpu.make_async_remote_copy(
            src_ref=piece(t), dst_ref=cols_ref.at[me],
            send_sem=send_sems.at[t], recv_sem=recv_sems.at[me],
            device_id=dev, device_id_type=pl.DeviceIdType.MESH)
        c.start()
        e = pltpu.make_async_remote_copy(
            src_ref=en_ref, dst_ref=en_all_ref.at[me],
            send_sem=en_send.at[t], recv_sem=en_recv.at[me],
            device_id=dev, device_id_type=pl.DeviceIdType.MESH)
        sends.append((c, e))
    for c, e in sends:
        e.start()
    for k in range(1, n):
        s = jnp.bitwise_xor(me, k)
        dev = (s, col, slab)
        pltpu.make_async_remote_copy(
            src_ref=piece(me), dst_ref=cols_ref.at[s],
            send_sem=send_sems.at[s], recv_sem=recv_sems.at[s],
            device_id=dev, device_id_type=pl.DeviceIdType.MESH).wait_recv()
        pltpu.make_async_remote_copy(
            src_ref=en_ref, dst_ref=en_all_ref.at[s],
            send_sem=en_send.at[s], recv_sem=en_recv.at[s],
            device_id=dev, device_id_type=pl.DeviceIdType.MESH).wait_recv()
    for c, e in sends:
        c.wait_send()
        e.wait_send()
    local.wait()
    local_en.wait()


def exchange(jacobian, local_energy, n):
    rows, slabs, cols = jacobian.shape
    width = cols // n
    en = local_energy.reshape(1, rows)
    return pl.pallas_call(
        functools.partial(exchange_kernel, n, width),
        out_shape=(
            jax.ShapeDtypeStruct((n, rows, slabs, width), jacobian.dtype),
            jax.ShapeDtypeStruct((n, 1, rows), local_energy.dtype),
        ),
        in_specs=[pl.BlockSpec(memory_space=pl.ANY)] * 2,
        out_specs=(pl.BlockSpec(memory_space=pl.ANY), pl.BlockSpec(memory_space=pl.ANY)),
        scratch_shapes=[
            pltpu.SemaphoreType.DMA((n,)),
            pltpu.SemaphoreType.DMA((n,)),
            pltpu.SemaphoreType.DMA((n,)),
            pltpu.SemaphoreType.DMA((n,)),
            pltpu.SemaphoreType.DMA((2,)),
        ],
        compiler_params=pltpu.CompilerParams(collective_id=0, has_side_effects=True),
    )(jacobian, en)


def reduce_kernel(n, parts, p_ref, out_ref, rs_buf, ar_buf, acc_ref, rs_send, rs_recv,
                  ar_send, ar_recv, ag_send, ag_recv, local_sem):
    me = lax.axis_index("smp")
    col = lax.axis_index("col")
    slab = lax.axis_index("slab")
    cs = col * 2 + slab
    mesh_id = pl.DeviceIdType.MESH

    def peer(k):
        return jnp.bitwise_xor(me, jnp.where(col == 0, k, n - k))

    barrier = pltpu.get_barrier_semaphore()
    for k in range(1, n):
        pl.semaphore_signal(barrier, inc=1, device_id=(jnp.bitwise_xor(me, k), col, slab),
                            device_id_type=mesh_id)
    for k in range(1, parts):
        other = jnp.bitwise_xor(cs, k)
        pl.semaphore_signal(barrier, inc=1, device_id=(me, other // 2, other % 2),
                            device_id_type=mesh_id)
    pl.semaphore_wait(barrier, n - 1 + parts - 1)

    sends = []
    for k in range(1, n):
        t = peer(k)
        c = pltpu.make_async_remote_copy(
            src_ref=p_ref.at[t], dst_ref=rs_buf.at[me], send_sem=rs_send.at[t],
            recv_sem=rs_recv.at[me], device_id=(t, col, slab), device_id_type=mesh_id)
        c.start()
        sends.append(c)
    rs_buf[pl.ds(me, 1)] = p_ref[pl.ds(me, 1)]
    for k in range(1, n):
        s = jnp.bitwise_xor(me, k)
        pltpu.make_async_remote_copy(
            src_ref=p_ref.at[s], dst_ref=rs_buf.at[s], send_sem=rs_send.at[s],
            recv_sem=rs_recv.at[s], device_id=(s, col, slab), device_id_type=mesh_id).wait_recv()
    total = rs_buf[0]
    for s in range(1, n):
        total = total + rs_buf[s]
    ar_buf[pl.ds(cs, 1)] = total[None]
    for k in range(1, parts):
        other = jnp.bitwise_xor(cs, k)
        c = pltpu.make_async_remote_copy(
            src_ref=ar_buf.at[cs], dst_ref=ar_buf.at[cs], send_sem=ar_send.at[other],
            recv_sem=ar_recv.at[cs], device_id=(me, other // 2, other % 2), device_id_type=mesh_id)
        c.start()
        sends.append(c)
    for k in range(1, parts):
        other = jnp.bitwise_xor(cs, k)
        pltpu.make_async_remote_copy(
            src_ref=ar_buf.at[other], dst_ref=ar_buf.at[other], send_sem=ar_send.at[other],
            recv_sem=ar_recv.at[other], device_id=(me, other // 2, other % 2),
            device_id_type=mesh_id).wait_recv()
    total = ar_buf[0]
    for j in range(1, parts):
        total = total + ar_buf[j]
    acc_ref[...] = total
    local = pltpu.make_async_copy(acc_ref, out_ref.at[me], local_sem.at[0])
    local.start()
    for k in range(1, n):
        t = peer(k)
        c = pltpu.make_async_remote_copy(
            src_ref=acc_ref, dst_ref=out_ref.at[me], send_sem=ag_send.at[t],
            recv_sem=ag_recv.at[me], device_id=(t, col, slab), device_id_type=mesh_id)
        c.start()
        sends.append(c)
    for k in range(1, n):
        s = jnp.bitwise_xor(me, k)
        pltpu.make_async_remote_copy(
            src_ref=acc_ref, dst_ref=out_ref.at[s], send_sem=ag_send.at[s],
            recv_sem=ag_recv.at[s], device_id=(s, col, slab), device_id_type=mesh_id).wait_recv()
    for c in sends:
        c.wait_send()
    local.wait()


def lower_psum(partial, n, parts, block=128):
    size = partial.shape[0]
    nb = size // block
    pairs = [(i, j) for i in range(nb) for j in range(i + 1)]
    packed = jnp.concatenate(
        [partial[i * block:(i + 1) * block, j * block:(j + 1) * block] for i, j in pairs], axis=0)
    rows = packed.shape[0] // n
    packed = packed.reshape(n, rows, block)
    reduced = pl.pallas_call(
        functools.partial(reduce_kernel, n, parts),
        out_shape=jax.ShapeDtypeStruct((n, rows, block), jnp.float32),
        in_specs=[pl.BlockSpec(memory_space=pltpu.VMEM)],
        out_specs=pl.BlockSpec(memory_space=pl.ANY),
        scratch_shapes=[
            pltpu.VMEM((n, rows, block), jnp.float32),
            pltpu.VMEM((parts, rows, block), jnp.float32),
            pltpu.VMEM((rows, block), jnp.float32),
            pltpu.SemaphoreType.DMA((n,)),
            pltpu.SemaphoreType.DMA((n,)),
            pltpu.SemaphoreType.DMA((parts,)),
            pltpu.SemaphoreType.DMA((parts,)),
            pltpu.SemaphoreType.DMA((n,)),
            pltpu.SemaphoreType.DMA((n,)),
            pltpu.SemaphoreType.DMA((1,)),
        ],
        compiler_params=pltpu.CompilerParams(collective_id=1, has_side_effects=True),
    )(packed)
    blocks = reduced.reshape(len(pairs), block, block)
    where = {p: k for k, p in enumerate(pairs)}
    zero = jnp.zeros((block, block), jnp.float32)
    lower = jnp.concatenate([
        jnp.concatenate([blocks[where[(i, j)]] if j <= i else zero for j in range(nb)], axis=1)
        for i in range(nb)], axis=0)
    diag = jnp.stack([blocks[where[(i, i)]] for i in range(nb)])
    return lower, diag


def cholesky_solve(a, rhs, block=128):
    n = a.shape[0]
    nb = n // block
    hi = lax.Precision.HIGHEST
    eye = jnp.eye(block, dtype=jnp.float32)
    inverses, panels, factors = [], [], []
    for k in range(nb):
        lo = k * block
        lkk = lax.linalg.cholesky(a[lo:lo + block, lo:lo + block], symmetrize_input=False)
        inv = lax.linalg.triangular_solve(lkk, eye, left_side=True, lower=True)
        factors.append(lkk)
        inverses.append(inv)
        if k < nb - 1:
            panel = jnp.dot(a[lo + block:, lo:lo + block], inv.T, precision=hi)
            panels.append(panel)
            a = a.at[lo + block:, lo + block:].add(-jnp.dot(panel, panel.T, precision=hi))
    ys = []
    tail = rhs
    for k in range(nb):
        y = jnp.dot(inverses[k], tail[:block], precision=hi)
        ys.append(y)
        if k < nb - 1:
            tail = tail[block:] - jnp.dot(panels[k], y, precision=hi)
    solved = jnp.dot(ys[nb - 1], inverses[nb - 1], precision=hi)
    for k in reversed(range(nb - 1)):
        r = ys[k] - jnp.dot(solved, panels[k], precision=hi)
        solved = jnp.concatenate([jnp.dot(r, inverses[k], precision=hi), solved])
    return solved


def shards(n, jacobian, local_energy):
    gathered, energies = exchange(jacobian, local_energy, n)
    energies = energies.reshape(-1)
    samples = energies.shape[0]
    root_count = jnp.sqrt(jnp.float32(samples))
    eps = (energies - jnp.mean(energies)) / root_count
    columns = gathered.reshape(samples, gathered.shape[2], gathered.shape[3])
    slab_count = columns.shape[1]
    width = columns.shape[2]
    values = columns.astype(jnp.float32)
    mean_row = jnp.mean(values, axis=0, keepdims=True)
    centered = (
        ((values - mean_row) / root_count).astype(jnp.bfloat16).reshape(samples, slab_count * width)
    )
    partial_gram = jnp.dot(centered, centered.T, preferred_element_type=jnp.float32)
    parts = lax.psum(1, ("col", "slab"))
    gram, diag = lower_psum(partial_gram, n, parts)
    shift = 0.01 * jnp.trace(gram) / samples
    coeffs = cholesky_solve(gram + shift * jnp.eye(samples, dtype=jnp.float32), eps)
    delta = jnp.sum(coeffs[:, None] * centered.astype(jnp.float32), axis=0)
    hi = lax.Precision.HIGHEST
    blocked = coeffs.reshape(diag.shape[0], diag.shape[1])
    full_c = (jnp.dot(gram, coeffs, precision=hi) + jnp.dot(coeffs, gram, precision=hi)
              - jnp.einsum("bij,bj->bi", diag, blocked, precision=hi).reshape(-1))
    squared = jnp.dot(coeffs, full_c, precision=hi)
    limit = 0.3 * jnp.sqrt(jnp.float32(SLABS * SLAB_COLS))
    scaled = -jnp.minimum(1.0, limit / jnp.sqrt(squared)) * delta
    return scaled.reshape(slab_count, width)


def solution(mesh):
    in_specs = (P("smp", "slab", "col"), P("smp"))
    out_specs = P("slab", ("col", "smp"))
    return jax.shard_map(functools.partial(shards, mesh.shape["smp"]), mesh=mesh,
                         in_specs=in_specs, out_specs=out_specs, check_vma=False)
```

```python
import functools

import jax
import jax.numpy as jnp
from jax import lax
from jax.experimental import pallas as pl
from jax.experimental.pallas import tpu as pltpu
from jax.sharding import PartitionSpec as P

SLABS = 32
SLAB_COLS = 16384


def exchange_kernel(n, width, jac_ref, en_ref, cols_ref, en_all_ref,
                    send_sems, recv_sems, en_send, en_recv, local_sems):
    me = lax.axis_index("smp")
    col = lax.axis_index("col")
    slab = lax.axis_index("slab")

    def piece(t):
        return jac_ref.at[:, :, pl.ds(pl.multiple_of(t * width, width), width)]

    barrier = pltpu.get_barrier_semaphore()
    for k in range(1, n):
        pl.semaphore_signal(barrier, inc=1, device_id=(jnp.bitwise_xor(me, k), col, slab),
                            device_id_type=pl.DeviceIdType.MESH)
    pl.semaphore_wait(barrier, n - 1)
    local = pltpu.make_async_copy(piece(me), cols_ref.at[me], local_sems.at[0])
    local_en = pltpu.make_async_copy(en_ref, en_all_ref.at[me], local_sems.at[1])
    sends = []
    order = [i ^ (i // 2) for i in range(1, n)]
    for i in range(n - 1):
        t = jnp.bitwise_xor(me, jnp.where(col == 0, order[i], order[n - 2 - i]))
        dev = (t, col, slab)
        c = pltpu.make_async_remote_copy(
            src_ref=piece(t), dst_ref=cols_ref.at[me],
            send_sem=send_sems.at[t], recv_sem=recv_sems.at[me],
            device_id=dev, device_id_type=pl.DeviceIdType.MESH)
        c.start()
        e = pltpu.make_async_remote_copy(
            src_ref=en_ref, dst_ref=en_all_ref.at[me],
            send_sem=en_send.at[t], recv_sem=en_recv.at[me],
            device_id=dev, device_id_type=pl.DeviceIdType.MESH)
        e.start()
        sends.append((c, e))
    local.start()
    local_en.start()
    for k in range(1, n):
        s = jnp.bitwise_xor(me, k)
        dev = (s, col, slab)
        pltpu.make_async_remote_copy(
            src_ref=piece(me), dst_ref=cols_ref.at[s],
            send_sem=send_sems.at[s], recv_sem=recv_sems.at[s],
            device_id=dev, device_id_type=pl.DeviceIdType.MESH).wait_recv()
        pltpu.make_async_remote_copy(
            src_ref=en_ref, dst_ref=en_all_ref.at[s],
            send_sem=en_send.at[s], recv_sem=en_recv.at[s],
            device_id=dev, device_id_type=pl.DeviceIdType.MESH).wait_recv()
    for c, e in sends:
        c.wait_send()
        e.wait_send()
    local.wait()
    local_en.wait()


def exchange(jacobian, local_energy, n):
    rows, slabs, cols = jacobian.shape
    width = cols // n
    en = local_energy.reshape(1, rows)
    return pl.pallas_call(
        functools.partial(exchange_kernel, n, width),
        out_shape=(
            jax.ShapeDtypeStruct((n, rows, slabs, width), jacobian.dtype),
            jax.ShapeDtypeStruct((n, 1, rows), local_energy.dtype),
        ),
        in_specs=[pl.BlockSpec(memory_space=pl.ANY)] * 2,
        out_specs=(pl.BlockSpec(memory_space=pl.ANY), pl.BlockSpec(memory_space=pl.ANY)),
        scratch_shapes=[
            pltpu.SemaphoreType.DMA((n,)),
            pltpu.SemaphoreType.DMA((n,)),
            pltpu.SemaphoreType.DMA((n,)),
            pltpu.SemaphoreType.DMA((n,)),
            pltpu.SemaphoreType.DMA((2,)),
        ],
        compiler_params=pltpu.CompilerParams(collective_id=0, has_side_effects=True),
    )(jacobian, en)


def reduce_kernel(n, parts, p_ref, out_ref, rs_buf, ar_buf, acc_ref, rs_send, rs_recv,
                  ar_send, ar_recv, ag_send, ag_recv, local_sem):
    me = lax.axis_index("smp")
    col = lax.axis_index("col")
    slab = lax.axis_index("slab")
    cs = col * 2 + slab
    mesh_id = pl.DeviceIdType.MESH

    def peer(k):
        return jnp.bitwise_xor(me, jnp.where(col == 0, k, n - k))

    barrier = pltpu.get_barrier_semaphore()
    for k in range(1, n):
        pl.semaphore_signal(barrier, inc=1, device_id=(jnp.bitwise_xor(me, k), col, slab),
                            device_id_type=mesh_id)
    for k in range(1, parts):
        other = jnp.bitwise_xor(cs, k)
        pl.semaphore_signal(barrier, inc=1, device_id=(me, other // 2, other % 2),
                            device_id_type=mesh_id)
    pl.semaphore_wait(barrier, n - 1 + parts - 1)

    sends = []
    for k in range(1, n):
        t = peer(k)
        c = pltpu.make_async_remote_copy(
            src_ref=p_ref.at[t], dst_ref=rs_buf.at[me], send_sem=rs_send.at[t],
            recv_sem=rs_recv.at[me], device_id=(t, col, slab), device_id_type=mesh_id)
        c.start()
        sends.append(c)
    rs_buf[pl.ds(me, 1)] = p_ref[pl.ds(me, 1)]
    for k in range(1, n):
        s = jnp.bitwise_xor(me, k)
        pltpu.make_async_remote_copy(
            src_ref=p_ref.at[s], dst_ref=rs_buf.at[s], send_sem=rs_send.at[s],
            recv_sem=rs_recv.at[s], device_id=(s, col, slab), device_id_type=mesh_id).wait_recv()
    total = rs_buf[0]
    for s in range(1, n):
        total = total + rs_buf[s]
    ar_buf[pl.ds(cs, 1)] = total[None]
    for k in range(1, parts):
        other = jnp.bitwise_xor(cs, k)
        c = pltpu.make_async_remote_copy(
            src_ref=ar_buf.at[cs], dst_ref=ar_buf.at[cs], send_sem=ar_send.at[other],
            recv_sem=ar_recv.at[cs], device_id=(me, other // 2, other % 2), device_id_type=mesh_id)
        c.start()
        sends.append(c)
    for k in range(1, parts):
        other = jnp.bitwise_xor(cs, k)
        pltpu.make_async_remote_copy(
            src_ref=ar_buf.at[other], dst_ref=ar_buf.at[other], send_sem=ar_send.at[other],
            recv_sem=ar_recv.at[other], device_id=(me, other // 2, other % 2),
            device_id_type=mesh_id).wait_recv()
    total = ar_buf[0]
    for j in range(1, parts):
        total = total + ar_buf[j]
    acc_ref[...] = total
    local = pltpu.make_async_copy(acc_ref, out_ref.at[me], local_sem.at[0])
    local.start()
    for k in range(1, n):
        t = peer(k)
        c = pltpu.make_async_remote_copy(
            src_ref=acc_ref, dst_ref=out_ref.at[me], send_sem=ag_send.at[t],
            recv_sem=ag_recv.at[me], device_id=(t, col, slab), device_id_type=mesh_id)
        c.start()
        sends.append(c)
    for k in range(1, n):
        s = jnp.bitwise_xor(me, k)
        pltpu.make_async_remote_copy(
            src_ref=acc_ref, dst_ref=out_ref.at[s], send_sem=ag_send.at[s],
            recv_sem=ag_recv.at[s], device_id=(s, col, slab), device_id_type=mesh_id).wait_recv()
    for c in sends:
        c.wait_send()
    local.wait()


def lower_psum(partial, n, parts, block=128):
    size = partial.shape[0]
    nb = size // block
    pairs = [(i, j) for i in range(nb) for j in range(i + 1)]
    packed = jnp.concatenate(
        [partial[i * block:(i + 1) * block, j * block:(j + 1) * block] for i, j in pairs], axis=0)
    rows = packed.shape[0] // n
    packed = packed.reshape(n, rows, block)
    reduced = pl.pallas_call(
        functools.partial(reduce_kernel, n, parts),
        out_shape=jax.ShapeDtypeStruct((n, rows, block), jnp.float32),
        in_specs=[pl.BlockSpec(memory_space=pltpu.VMEM)],
        out_specs=pl.BlockSpec(memory_space=pl.ANY),
        scratch_shapes=[
            pltpu.VMEM((n, rows, block), jnp.float32),
            pltpu.VMEM((parts, rows, block), jnp.float32),
            pltpu.VMEM((rows, block), jnp.float32),
            pltpu.SemaphoreType.DMA((n,)),
            pltpu.SemaphoreType.DMA((n,)),
            pltpu.SemaphoreType.DMA((parts,)),
            pltpu.SemaphoreType.DMA((parts,)),
            pltpu.SemaphoreType.DMA((n,)),
            pltpu.SemaphoreType.DMA((n,)),
            pltpu.SemaphoreType.DMA((1,)),
        ],
        compiler_params=pltpu.CompilerParams(collective_id=1, has_side_effects=True),
    )(packed)
    blocks = reduced.reshape(len(pairs), block, block)
    where = {p: k for k, p in enumerate(pairs)}
    zero = jnp.zeros((block, block), jnp.float32)
    lower = jnp.concatenate([
        jnp.concatenate([blocks[where[(i, j)]] if j <= i else zero for j in range(nb)], axis=1)
        for i in range(nb)], axis=0)
    diag = jnp.stack([blocks[where[(i, i)]] for i in range(nb)])
    return lower, diag


def cholesky_solve(a, rhs, block=128):
    n = a.shape[0]
    nb = n // block
    hi = lax.Precision.HIGHEST
    eye = jnp.eye(block, dtype=jnp.float32)
    inverses, panels, factors = [], [], []
    for k in range(nb):
        lo = k * block
        lkk = lax.linalg.cholesky(a[lo:lo + block, lo:lo + block], symmetrize_input=False)
        inv = lax.linalg.triangular_solve(lkk, eye, left_side=True, lower=True)
        factors.append(lkk)
        inverses.append(inv)
        if k < nb - 1:
            panel = jnp.dot(a[lo + block:, lo:lo + block], inv.T, precision=hi)
            panels.append(panel)
            a = a.at[lo + block:, lo + block:].add(-jnp.dot(panel, panel.T, precision=hi))
    ys = []
    tail = rhs
    for k in range(nb):
        y = jnp.dot(inverses[k], tail[:block], precision=hi)
        ys.append(y)
        if k < nb - 1:
            tail = tail[block:] - jnp.dot(panels[k], y, precision=hi)
    solved = jnp.dot(ys[nb - 1], inverses[nb - 1], precision=hi)
    for k in reversed(range(nb - 1)):
        r = ys[k] - jnp.dot(solved, panels[k], precision=hi)
        solved = jnp.concatenate([jnp.dot(r, inverses[k], precision=hi), solved])
    return solved


def shards(n, jacobian, local_energy):
    gathered, energies = exchange(jacobian, local_energy, n)
    energies = energies.reshape(-1)
    samples = energies.shape[0]
    root_count = jnp.sqrt(jnp.float32(samples))
    eps = (energies - jnp.mean(energies)) / root_count
    columns = gathered.reshape(samples, gathered.shape[2], gathered.shape[3])
    slab_count = columns.shape[1]
    width = columns.shape[2]
    values = columns.astype(jnp.float32)
    mean_row = jnp.mean(values, axis=0, keepdims=True)
    centered = (
        ((values - mean_row) / root_count).astype(jnp.bfloat16).reshape(samples, slab_count * width)
    )
    partial_gram = jnp.dot(centered, centered.T, preferred_element_type=jnp.float32)
    parts = lax.psum(1, ("col", "slab"))
    gram, diag = lower_psum(partial_gram, n, parts)
    shift = 0.01 * jnp.trace(gram) / samples
    coeffs = cholesky_solve(gram + shift * jnp.eye(samples, dtype=jnp.float32), eps)
    delta = jnp.sum(coeffs[:, None] * centered.astype(jnp.float32), axis=0)
    hi = lax.Precision.HIGHEST
    blocked = coeffs.reshape(diag.shape[0], diag.shape[1])
    full_c = (jnp.dot(gram, coeffs, precision=hi) + jnp.dot(coeffs, gram, precision=hi)
              - jnp.einsum("bij,bj->bi", diag, blocked, precision=hi).reshape(-1))
    squared = jnp.dot(coeffs, full_c, precision=hi)
    limit = 0.3 * jnp.sqrt(jnp.float32(SLABS * SLAB_COLS))
    scaled = -jnp.minimum(1.0, limit / jnp.sqrt(squared)) * delta
    return scaled.reshape(slab_count, width)


def solution(mesh):
    in_specs = (P("smp", "slab", "col"), P("smp"))
    out_specs = P("slab", ("col", "smp"))
    return jax.shard_map(functools.partial(shards, mesh.shape["smp"]), mesh=mesh,
                         in_specs=in_specs, out_specs=out_specs, check_vma=False)
```

```python
import functools

import jax
import jax.numpy as jnp
from jax import lax
from jax.experimental import pallas as pl
from jax.experimental.pallas import tpu as pltpu
from jax.sharding import PartitionSpec as P

SLABS = 32
SLAB_COLS = 16384


def exchange_kernel(n, width, jac_ref, en_ref, cols_ref, en_all_ref,
                    send_sems, recv_sems, en_send, en_recv, local_sems):
    me = lax.axis_index("smp")
    col = lax.axis_index("col")
    slab = lax.axis_index("slab")

    def piece(t):
        return jac_ref.at[:, :, pl.ds(pl.multiple_of(t * width, width), width)]

    barrier = pltpu.get_barrier_semaphore()
    for k in range(1, n):
        pl.semaphore_signal(barrier, inc=1, device_id=(jnp.bitwise_xor(me, k), col, slab),
                            device_id_type=pl.DeviceIdType.MESH)
    pl.semaphore_wait(barrier, n - 1)
    local = pltpu.make_async_copy(piece(me), cols_ref.at[me], local_sems.at[0])
    local.start()
    local_en = pltpu.make_async_copy(en_ref, en_all_ref.at[me], local_sems.at[1])
    local_en.start()
    sends = []
    order = [i ^ (i // 2) for i in range(1, n)]
    for i in range(n - 1):
        t = jnp.bitwise_xor(me, jnp.where(col == 0, order[i], order[n - 2 - i]))
        dev = (t, col, slab)
        c = pltpu.make_async_remote_copy(
            src_ref=piece(t), dst_ref=cols_ref.at[me],
            send_sem=send_sems.at[t], recv_sem=recv_sems.at[me],
            device_id=dev, device_id_type=pl.DeviceIdType.MESH)
        c.start()
        e = pltpu.make_async_remote_copy(
            src_ref=en_ref, dst_ref=en_all_ref.at[me],
            send_sem=en_send.at[t], recv_sem=en_recv.at[me],
            device_id=dev, device_id_type=pl.DeviceIdType.MESH)
        e.start()
        sends.append((c, e))
    for k in range(1, n):
        s = jnp.bitwise_xor(me, k)
        dev = (s, col, slab)
        pltpu.make_async_remote_copy(
            src_ref=piece(me), dst_ref=cols_ref.at[s],
            send_sem=send_sems.at[s], recv_sem=recv_sems.at[s],
            device_id=dev, device_id_type=pl.DeviceIdType.MESH).wait_recv()
        pltpu.make_async_remote_copy(
            src_ref=en_ref, dst_ref=en_all_ref.at[s],
            send_sem=en_send.at[s], recv_sem=en_recv.at[s],
            device_id=dev, device_id_type=pl.DeviceIdType.MESH).wait_recv()
    for c, e in sends:
        c.wait_send()
        e.wait_send()
    local.wait()
    local_en.wait()


def exchange(jacobian, local_energy, n):
    rows, slabs, cols = jacobian.shape
    width = cols // n
    en = local_energy.reshape(1, rows)
    return pl.pallas_call(
        functools.partial(exchange_kernel, n, width),
        out_shape=(
            jax.ShapeDtypeStruct((n, rows, slabs, width), jacobian.dtype),
            jax.ShapeDtypeStruct((n, 1, rows), local_energy.dtype),
        ),
        in_specs=[pl.BlockSpec(memory_space=pl.ANY)] * 2,
        out_specs=(pl.BlockSpec(memory_space=pl.ANY), pl.BlockSpec(memory_space=pl.ANY)),
        scratch_shapes=[
            pltpu.SemaphoreType.DMA((n,)),
            pltpu.SemaphoreType.DMA((n,)),
            pltpu.SemaphoreType.DMA((n,)),
            pltpu.SemaphoreType.DMA((n,)),
            pltpu.SemaphoreType.DMA((2,)),
        ],
        compiler_params=pltpu.CompilerParams(collective_id=0, has_side_effects=True),
    )(jacobian, en)


def reduce_kernel(n, parts, p_ref, out_ref, rs_buf, ar_buf, acc_ref, rs_send, rs_recv,
                  ar_send, ar_recv, ag_send, ag_recv, local_sem):
    me = lax.axis_index("smp")
    col = lax.axis_index("col")
    slab = lax.axis_index("slab")
    cs = col * 2 + slab
    mesh_id = pl.DeviceIdType.MESH

    def peer(k):
        return jnp.bitwise_xor(me, jnp.where(col == 0, k, n - k))

    barrier = pltpu.get_barrier_semaphore()
    for k in range(1, n):
        pl.semaphore_signal(barrier, inc=1, device_id=(jnp.bitwise_xor(me, k), col, slab),
                            device_id_type=mesh_id)
    for k in range(1, parts):
        other = jnp.bitwise_xor(cs, k)
        pl.semaphore_signal(barrier, inc=1, device_id=(me, other // 2, other % 2),
                            device_id_type=mesh_id)
    pl.semaphore_wait(barrier, n - 1 + parts - 1)

    sends = []
    for k in range(1, n):
        t = peer(k)
        c = pltpu.make_async_remote_copy(
            src_ref=p_ref.at[t], dst_ref=rs_buf.at[me], send_sem=rs_send.at[t],
            recv_sem=rs_recv.at[me], device_id=(t, col, slab), device_id_type=mesh_id)
        c.start()
        sends.append(c)
    own = pltpu.make_async_copy(p_ref.at[me], rs_buf.at[me], local_sem.at[1])
    own.start()
    for k in range(1, n):
        s = jnp.bitwise_xor(me, k)
        pltpu.make_async_remote_copy(
            src_ref=p_ref.at[s], dst_ref=rs_buf.at[s], send_sem=rs_send.at[s],
            recv_sem=rs_recv.at[s], device_id=(s, col, slab), device_id_type=mesh_id).wait_recv()
    own.wait()
    total = rs_buf[0]
    for s in range(1, n):
        total = total + rs_buf[s]
    ar_buf[pl.ds(cs, 1)] = total[None]
    for k in range(1, parts):
        other = jnp.bitwise_xor(cs, k)
        c = pltpu.make_async_remote_copy(
            src_ref=ar_buf.at[cs], dst_ref=ar_buf.at[cs], send_sem=ar_send.at[other],
            recv_sem=ar_recv.at[cs], device_id=(me, other // 2, other % 2), device_id_type=mesh_id)
        c.start()
        sends.append(c)
    for k in range(1, parts):
        other = jnp.bitwise_xor(cs, k)
        pltpu.make_async_remote_copy(
            src_ref=ar_buf.at[other], dst_ref=ar_buf.at[other], send_sem=ar_send.at[other],
            recv_sem=ar_recv.at[other], device_id=(me, other // 2, other % 2),
            device_id_type=mesh_id).wait_recv()
    total = ar_buf[0]
    for j in range(1, parts):
        total = total + ar_buf[j]
    acc_ref[...] = total
    local = pltpu.make_async_copy(acc_ref, out_ref.at[me], local_sem.at[0])
    local.start()
    for k in range(1, n):
        t = peer(k)
        c = pltpu.make_async_remote_copy(
            src_ref=acc_ref, dst_ref=out_ref.at[me], send_sem=ag_send.at[t],
            recv_sem=ag_recv.at[me], device_id=(t, col, slab), device_id_type=mesh_id)
        c.start()
        sends.append(c)
    for k in range(1, n):
        s = jnp.bitwise_xor(me, k)
        pltpu.make_async_remote_copy(
            src_ref=acc_ref, dst_ref=out_ref.at[s], send_sem=ag_send.at[s],
            recv_sem=ag_recv.at[s], device_id=(s, col, slab), device_id_type=mesh_id).wait_recv()
    for c in sends:
        c.wait_send()
    local.wait()


def lower_psum(partial, n, parts, block=128):
    size = partial.shape[0]
    nb = size // block
    pairs = [(i, j) for i in range(nb) for j in range(i + 1)]
    packed = jnp.concatenate(
        [partial[i * block:(i + 1) * block, j * block:(j + 1) * block] for i, j in pairs], axis=0)
    rows = packed.shape[0] // n
    packed = packed.reshape(n, rows, block)
    reduced = pl.pallas_call(
        functools.partial(reduce_kernel, n, parts),
        out_shape=jax.ShapeDtypeStruct((n, rows, block), jnp.float32),
        in_specs=[pl.BlockSpec(memory_space=pl.ANY)],
        out_specs=pl.BlockSpec(memory_space=pl.ANY),
        scratch_shapes=[
            pltpu.VMEM((n, rows, block), jnp.float32),
            pltpu.VMEM((parts, rows, block), jnp.float32),
            pltpu.VMEM((rows, block), jnp.float32),
            pltpu.SemaphoreType.DMA((n,)),
            pltpu.SemaphoreType.DMA((n,)),
            pltpu.SemaphoreType.DMA((parts,)),
            pltpu.SemaphoreType.DMA((parts,)),
            pltpu.SemaphoreType.DMA((n,)),
            pltpu.SemaphoreType.DMA((n,)),
            pltpu.SemaphoreType.DMA((2,)),
        ],
        compiler_params=pltpu.CompilerParams(collective_id=1, has_side_effects=True),
    )(packed)
    blocks = reduced.reshape(len(pairs), block, block)
    where = {p: k for k, p in enumerate(pairs)}
    zero = jnp.zeros((block, block), jnp.float32)
    lower = jnp.concatenate([
        jnp.concatenate([blocks[where[(i, j)]] if j <= i else zero for j in range(nb)], axis=1)
        for i in range(nb)], axis=0)
    diag = jnp.stack([blocks[where[(i, i)]] for i in range(nb)])
    return lower, diag


def cholesky_solve(a, rhs, block=128):
    n = a.shape[0]
    nb = n // block
    hi = lax.Precision.HIGHEST
    eye = jnp.eye(block, dtype=jnp.float32)
    inverses, panels, factors = [], [], []
    for k in range(nb):
        lo = k * block
        lkk = lax.linalg.cholesky(a[lo:lo + block, lo:lo + block], symmetrize_input=False)
        inv = lax.linalg.triangular_solve(lkk, eye, left_side=True, lower=True)
        factors.append(lkk)
        inverses.append(inv)
        if k < nb - 1:
            panel = jnp.dot(a[lo + block:, lo:lo + block], inv.T, precision=hi)
            panels.append(panel)
            a = a.at[lo + block:, lo + block:].add(-jnp.dot(panel, panel.T, precision=hi))
    ys = []
    tail = rhs
    for k in range(nb):
        y = jnp.dot(inverses[k], tail[:block], precision=hi)
        ys.append(y)
        if k < nb - 1:
            tail = tail[block:] - jnp.dot(panels[k], y, precision=hi)
    solved = jnp.dot(ys[nb - 1], inverses[nb - 1], precision=hi)
    for k in reversed(range(nb - 1)):
        r = ys[k] - jnp.dot(solved, panels[k], precision=hi)
        solved = jnp.concatenate([jnp.dot(r, inverses[k], precision=hi), solved])
    return solved


def shards(n, jacobian, local_energy):
    gathered, energies = exchange(jacobian, local_energy, n)
    energies = energies.reshape(-1)
    samples = energies.shape[0]
    root_count = jnp.sqrt(jnp.float32(samples))
    eps = (energies - jnp.mean(energies)) / root_count
    columns = gathered.reshape(samples, gathered.shape[2], gathered.shape[3])
    slab_count = columns.shape[1]
    width = columns.shape[2]
    values = columns.astype(jnp.float32)
    mean_row = jnp.mean(values, axis=0, keepdims=True)
    centered = (
        ((values - mean_row) / root_count).astype(jnp.bfloat16).reshape(samples, slab_count * width)
    )
    partial_gram = jnp.dot(centered, centered.T, preferred_element_type=jnp.float32)
    parts = lax.psum(1, ("col", "slab"))
    gram, diag = lower_psum(partial_gram, n, parts)
    shift = 0.01 * jnp.trace(gram) / samples
    coeffs = cholesky_solve(gram + shift * jnp.eye(samples, dtype=jnp.float32), eps)
    delta = jnp.sum(coeffs[:, None] * centered.astype(jnp.float32), axis=0)
    hi = lax.Precision.HIGHEST
    blocked = coeffs.reshape(diag.shape[0], diag.shape[1])
    full_c = (jnp.dot(gram, coeffs, precision=hi) + jnp.dot(coeffs, gram, precision=hi)
              - jnp.einsum("bij,bj->bi", diag, blocked, precision=hi).reshape(-1))
    squared = jnp.dot(coeffs, full_c, precision=hi)
    limit = 0.3 * jnp.sqrt(jnp.float32(SLABS * SLAB_COLS))
    scaled = -jnp.minimum(1.0, limit / jnp.sqrt(squared)) * delta
    return scaled.reshape(slab_count, width)


def solution(mesh):
    in_specs = (P("smp", "slab", "col"), P("smp"))
    out_specs = P("slab", ("col", "smp"))
    return jax.shard_map(functools.partial(shards, mesh.shape["smp"]), mesh=mesh,
                         in_specs=in_specs, out_specs=out_specs, check_vma=False)
```
